32 devices in a mesh: groups: 2 (over y), imp: 8 (over z, x), adv: 2 (over core).
Axes of the slice: x: 2, y: 2, z: 4, core: 2. Of those that a mesh axis runs over, the one named last changes fastest.
Arguments:
- imp_emb: bfloat16 [4096, 256], P(('groups', 'imp')), parts along dimension 0, may hold values from -6 to 6
- adv_emb: bfloat16 [8192, 256], P(('groups', 'imp', 'adv')), parts along dimension 0, may hold values from -6 to 6
- allowances: int32 [8192], P(('groups', 'imp', 'adv')), parts along dimension 0, may hold values from 1024 to 16383
- eligible_slots: int32 [32, 8], P(('groups', 'imp', 'adv')), parts along dimension 0, may hold values from -1 to 3, as said below
Outputs:
- prices: float32 [4096], P(('groups', 'imp')), parts along dimension 0
- utilities: float32 [8192], P(('groups', 'imp', 'adv')), parts along dimension 0
The draws below stay inside these ranges and needn't reach their ends.
There are 2 independent parts, one for each index of `groups`. The reference program is written for one: setup_inputs(seed, part) draws one part's arguments, and reference() takes and returns one part's arrays. A program takes and returns all parts, laid end to end along the dimension named above; each array names one. Nothing has to cross between parts.
Inputs may be any that keep to these rules, and one draw needn't show every extreme that they name: eligible_slots[d, i] is -1 or k * 2 + m with k < 2 and m < 2; every advertiser block is eligible with at least one impression block.
All inputs are finite; a program needn't handle non-finite values.
Results may differ from the reference program's by a relative error of at most 0.00081.
Values may be sent and summed in bfloat16 or wider, within the bound.
No kernel may reach another device: no remote copies, remote signals or barrier semaphores. Data moves between devices by JAX's collectives and lax.ppermute only.
A program may use at most 128 MiB of HBM per device.

```python
import math
import jax
import jax.numpy as jnp
from jax import lax

BLK = 128
EMB = 256
IB_DEV = 2
AB_DEV = 2
ITERS = 2
SLOTS = 8
OWNERS = 16
IMPRESSIONS = 2048
ADVERTISERS = 4096


def draw_eligible_slots(key, part):
    key_live = jax.random.fold_in(key, 11)
    key_adv = jax.random.fold_in(key, 12)
    key_imp = jax.random.fold_in(key, 13)
    live_roll = jax.random.randint(key_live, (OWNERS, SLOTS), 0, 8)
    live_draw = jnp.where(live_roll < 7, 1, 0)
    adv_draw = jax.random.randint(key_adv, (OWNERS, SLOTS), 0, AB_DEV)
    imp_draw = jax.random.randint(key_imp, (OWNERS, SLOTS), 0, IB_DEV)
    owner_home = jnp.arange(OWNERS, dtype=jnp.int32) // (OWNERS // SLOTS)
    home_ids = jnp.arange(SLOTS, dtype=jnp.int32)
    offset = (home_ids[None, :] - owner_home[:, None] - 1) % SLOTS
    forced = offset < AB_DEV
    adv_draw = jnp.where(forced, offset, adv_draw)
    live_draw = jnp.where(forced, 1, live_draw)
    slot_codes = jnp.where(live_draw == 1, adv_draw * IB_DEV + imp_draw, -1)
    return slot_codes.astype(jnp.int32)


def touch_ends(result, key, low, top_value):
    dims = result.shape
    spot = [jax.random.randint(jax.random.fold_in(key, axis), (), 0, dims[axis]) for axis in range(len(dims))]
    result = result.at[tuple(spot)].set(low)
    longest = dims.index(max(dims))
    spot[longest] = (spot[longest] + 1) % dims[longest]
    return result.at[tuple(spot)].set(top_value)


def level_of(key, extent, split, low, largest):
    factor_of = 1.0
    for dim, blocks in split:
        draws = jax.random.uniform(jax.random.fold_in(jax.random.fold_in(key, 6), dim), (blocks,), jnp.float32, low / len(split), largest / len(split))
        factor_of = factor_of * jnp.repeat(jnp.exp(draws), extent[dim] // blocks).reshape((-1,) + (1,) * (len(extent) - 1 - dim))
    return factor_of


def bell_draw(rng, dims, scale, bound, pieces=(), kind=jnp.bfloat16):
    values = scale * jax.random.normal(rng, dims, jnp.float32)
    if pieces:
        values = values * level_of(rng, dims, pieces, -0.22, 0.18)
    return jnp.clip(values, -bound, bound).astype(kind)


def setup_inputs(seed: int = 0, part: int = 0) -> dict:
    arg_keys = jax.random.split(jax.random.key(seed), 5)
    part_keys = jax.random.split(jax.random.fold_in(arg_keys[4], part), 5)
    return {
        "imp_emb": bell_draw(part_keys[0], (IMPRESSIONS, EMB), 1.0, 6.0, ((0, 8),)),
        "adv_emb": bell_draw(part_keys[1], (ADVERTISERS, EMB), 1.0, 6.0, ((0, 16),)),
        "allowances": touch_ends(jax.random.randint(part_keys[2], (ADVERTISERS,), 1024, 16384), jax.random.fold_in(part_keys[2], 1), 1024, 16383).astype(jnp.int32),
        "eligible_slots": draw_eligible_slots(jax.random.fold_in(jax.random.fold_in(arg_keys[4], part), 71), part),
    }


def owner_replay(owner_index, tables, imp_emb, adv_emb, allowances, eligible_slots):
    slot_codes = eligible_slots[owner_index]
    is_live = slot_codes >= 0
    clamped = jnp.maximum(slot_codes, 0)
    adv_pick = (clamped // IB_DEV).astype(jnp.int32)
    imp_pick = (clamped % IB_DEV).astype(jnp.int32)
    width = AB_DEV * BLK
    start = (owner_index * width).astype(jnp.int32)
    owner_rows = lax.dynamic_slice_in_dim(adv_emb, start, width, 0).reshape(AB_DEV, BLK, EMB)
    adv_rows = jnp.take(owner_rows, adv_pick, axis=0)
    home_slabs = imp_emb.reshape(SLOTS, IB_DEV, BLK, EMB)
    picked = jnp.take_along_axis(home_slabs, imp_pick[:, None, None, None], axis=1)[:, 0]
    scores = jnp.einsum('nae,nbe->nab', adv_rows.astype(jnp.float32), picked.astype(jnp.float32)) * (1.0 / math.sqrt(EMB))
    value_tiles = jnp.where(is_live[:, None, None], jax.nn.softplus(scores), 0.0).astype(jnp.bfloat16)
    spend_rows = lax.dynamic_slice_in_dim(allowances, start, width, 0).astype(jnp.float32).reshape(AB_DEV, BLK) / 1024.0
    block_ids = jnp.arange(AB_DEV, dtype=jnp.int32)
    picker = (adv_pick[:, None] == block_ids[None, :]).astype(jnp.float32)
    live_picker = picker * is_live[:, None].astype(jnp.float32)
    hp = lax.Precision.HIGHEST
    row_totals = lax.optimization_barrier(jnp.sum(value_tiles.astype(jnp.float32), axis=2))
    value_sums = jnp.einsum('nk,na->ka', live_picker, row_totals, precision=hp)
    slot_spend = jnp.einsum('nk,ka->na', live_picker, spend_rows, precision=hp)
    slot_sums = jnp.einsum('nk,ka->na', picker, value_sums, precision=hp)
    bid_tiles = (slot_spend / slot_sums)[:, :, None] * value_tiles.astype(jnp.float32)
    home_ids = jnp.arange(SLOTS, dtype=jnp.int32)
    utility = jnp.zeros((AB_DEV, BLK), jnp.float32)
    for price_grid in tables:
        slot_prices = price_grid[home_ids, imp_pick]
        divisor = jnp.where(is_live[:, None], slot_prices, 1.0)
        shares = bid_tiles / divisor[:, None, :]
        earned = value_tiles.astype(jnp.float32) * shares
        utility = jnp.einsum('nk,na->ka', live_picker, lax.optimization_barrier(jnp.sum(earned, axis=2)), precision=hp)
        slot_utility = jnp.einsum('nk,ka->na', picker, utility, precision=hp)
        bid_tiles = (slot_spend / slot_utility)[:, :, None] * earned
    totals = jnp.where(is_live[:, None], lax.optimization_barrier(jnp.sum(bid_tiles, axis=1)), 0.0)
    contribution = jnp.zeros((SLOTS, IB_DEV, BLK), jnp.float32).at[home_ids, imp_pick].add(totals)
    return (contribution, utility)

def reference(imp_emb, adv_emb, allowances, eligible_slots):
    tables = []
    utilities = None
    for round_index in range(ITERS + 1):
        known = tuple(tables)

        def visit_owner(running, owner_index):
            contribution, utility = owner_replay(owner_index, known, imp_emb, adv_emb, allowances, eligible_slots)
            return (running + contribution, utility)
        price_grid, utilities = lax.scan(visit_owner, jnp.zeros((SLOTS, IB_DEV, BLK), jnp.float32), jnp.arange(OWNERS, dtype=jnp.int32))
        tables.append(price_grid)
    return (tables[-1].reshape(IMPRESSIONS), utilities.reshape(ADVERTISERS))
```

```python
import functools
import math

import jax
import jax.numpy as jnp
from jax import lax
from jax.experimental import pallas as pl
from jax.experimental.pallas import tpu as pltpu
from jax.sharding import PartitionSpec as P

BLK = 128
EMB = 256
IB_DEV = 2
AB_DEV = 2
ITERS = 2
SMALL_IMP = 8
REP_BITS = (2, 4)
JOIN = True

F32 = jnp.float32
BF16 = jnp.bfloat16


def rows_to_column(row, eye):
    return jnp.sum(jnp.where(eye, jnp.broadcast_to(row, (BLK, BLK)), 0.0), axis=1, keepdims=True)


def column_to_row(col, eye):
    return jnp.sum(jnp.where(eye, jnp.broadcast_to(col, (BLK, BLK)), 0.0), axis=0, keepdims=True)


def make_eye():
    return lax.broadcasted_iota(jnp.int32, (BLK, BLK), 0) == lax.broadcasted_iota(
        jnp.int32, (BLK, BLK), 1
    )


def softplus(s):
    e = jnp.exp(-jnp.abs(s))
    near = e * (1.0 - e * (0.5 - e * (1.0 / 3.0 - e * 0.25)))
    return jnp.maximum(s, 0.0) + jnp.where(e < 0.01, near, jnp.log(1.0 + e))


def fold(tile):
    return jnp.sum(tile.reshape(BLK // 8, 8, BLK), axis=0)


def slot_of(codes, owner, home):
    code = codes[owner, home]
    clamped = jnp.maximum(code, 0)
    return code >= 0, lax.shift_right_logical(clamped, 1), lax.bitwise_and(clamped, 1)


def finish_prices(pacc, price_out, homes):
    for row in range(homes * IB_DEV):
        price_out[pl.ds(row, 1), :] = jnp.sum(pacc[row], axis=0, keepdims=True)


def take(refs, *counts):
    parts = []
    for n in counts:
        parts.append(refs[:n])
        refs = refs[n:]
    return (*parts, refs)


def read_codes(codes, code_refs, homes):
    me = lax.axis_index("imp")
    for o, ref in enumerate(code_refs):
        for m in range(homes):
            codes[o, m] = ref[AB_DEV, lax.bitwise_xor(me, m)]


def spend_column(notes, row, eye):
    part = notes[row // AB_DEV][pl.ds(row % AB_DEV, 1), :]
    return rows_to_column(part.astype(F32), eye) * (1.0 / 1024.0)


def first_kernel(owners, homes, *refs):
    code_refs, notes, (imp_own,), adv, mine, theirs, rest = take(
        refs, owners, owners, 1, owners, homes - 1, homes - 1
    )
    values, factor_out, price_out, codes, adv_s, imp_s, acc, fac, pacc = rest
    read_codes(codes, code_refs, homes)
    core = lax.axis_index("adv")
    wide = AB_DEV * BLK
    for o in range(owners):
        adv_s[pl.ds(o * wide, wide), :] = adv[o][...]
    imp_s[pl.ds(0, wide), :] = imp_own[...]
    for m in range(1, homes):
        imp_s[pl.ds(pl.multiple_of(m * wide + core * BLK, BLK), BLK), :] = mine[m - 1][...]
        imp_s[pl.ds(pl.multiple_of(m * wide + (1 - core) * BLK, BLK), BLK), :] = theirs[m - 1][...]
    acc[...] = jnp.zeros_like(acc)
    pacc[...] = jnp.zeros_like(pacc)
    eye = make_eye()

    def value_body(o, carry):
        for m in range(homes):
            live, k, b = slot_of(codes, o, m)
            lhs = adv_s[pl.ds(pl.multiple_of(o * wide + k * BLK, BLK), BLK), :]
            rhs = imp_s[pl.ds(pl.multiple_of(m * wide + b * BLK, BLK), BLK), :]
            s = lax.dot_general(
                lhs, rhs, (((1,), (1,)), ((), ())), preferred_element_type=F32
            ) * (1.0 / math.sqrt(EMB))
            v = jnp.where(live, softplus(s), 0.0).astype(BF16)
            values[o * homes + m] = v
            acc[o * AB_DEV + k] += v.astype(F32)
        return carry

    lax.fori_loop(0, owners, value_body, 0)
    for r in range(owners * AB_DEV):
        total = jnp.sum(acc[r], axis=1, keepdims=True)
        spend = spend_column(notes, r, eye)
        factor = spend / total
        fac[r] = jnp.broadcast_to(factor, (BLK, BLK))
        factor_out[pl.ds(r, 1), :] = column_to_row(factor, eye)

    def bid_body(o, carry):
        for m in range(homes):
            _, k, b = slot_of(codes, o, m)
            pacc[m * IB_DEV + b] += fold(fac[o * AB_DEV + k] * values[o * homes + m].astype(F32))
        return carry

    lax.fori_loop(0, owners, bid_body, 0)
    finish_prices(pacc, price_out, homes)


def add_prices(parts, homes):
    rows = []
    for m in range(homes):
        terms = [ref[pl.ds((m ^ d) * IB_DEV, IB_DEV), :] for d, ref in parts]
        while len(terms) > 1:
            terms = [terms[i] + terms[i + 1] for i in range(0, len(terms), 2)]
        rows.append(terms[0])
    return jnp.concatenate(rows, axis=0)


def next_kernel(owners, homes, rounds, last, spans, *refs):
    code_refs, notes, (values,), parts, old, factors, rest = take(
        refs, owners, owners, 1, len(spans), rounds - 1, rounds
    )
    if last:
        fresh_out, price_out, codes, earned_s, acc, fac, rps, pacc = rest
    else:
        fresh_out, price_out, full_out, codes, earned_s, acc, fac, rps, pacc = rest
    read_codes(codes, code_refs, homes)
    full = add_prices(list(zip(spans, parts)), homes)
    if not last:
        full_out[...] = full
    prices = [ref[...] for ref in old] + [full]
    acc[...] = jnp.zeros_like(acc)
    pacc[...] = jnp.zeros_like(pacc)
    eye = make_eye()
    for t in range(rounds):
        p = prices[t]
        rps[t] = jnp.where(p > 0.0, 1.0 / p, 1.0)
        for r in range(owners * AB_DEV):
            col = rows_to_column(factors[t][pl.ds(r, 1), :], eye)
            fac[t, r] = jnp.broadcast_to(col, (BLK, BLK))

    def earn_body(o, carry):
        for m in range(homes):
            _, k, b = slot_of(codes, o, m)
            v = values[o * homes + m].astype(F32)
            earned = v
            for t in range(rounds):
                share = (fac[t, o * AB_DEV + k] * earned) * rps[t, pl.ds(m * IB_DEV + b, 1), :]
                earned = v * share
            earned_s[o * homes + m] = earned
            acc[o * AB_DEV + k] += earned
        return carry

    lax.fori_loop(0, owners, earn_body, 0)
    for r in range(owners * AB_DEV):
        utility = jnp.sum(acc[r], axis=1, keepdims=True)
        spend = spend_column(notes, r, eye)
        factor = spend / utility
        fac[0, r] = jnp.broadcast_to(factor, (BLK, BLK))
        if not last:
            fresh_out[pl.ds(r, 1), :] = column_to_row(factor, eye)
        elif r < AB_DEV:
            fresh_out[pl.ds(r, 1), :] = column_to_row(utility, eye)

    def bid_body(o, carry):
        for m in range(homes):
            _, k, b = slot_of(codes, o, m)
            pacc[m * IB_DEV + b] += fold(fac[0, o * AB_DEV + k] * earned_s[o * homes + m])
        return carry

    lax.fori_loop(0, owners, bid_body, 0)
    finish_prices(pacc, price_out, homes)


def shaped(shape, dtype):
    return jax.ShapeDtypeStruct(shape, dtype)


SMEM = pl.BlockSpec(memory_space=pltpu.SMEM)
VMEM = pl.BlockSpec(memory_space=pltpu.VMEM)


LIMIT = 24 << 20


def run_first(owners, homes, notes, imp, adv, mine, theirs):
    tiles = owners * homes
    rows = owners * AB_DEV
    return pl.pallas_call(
        functools.partial(first_kernel, owners, homes),
        out_shape=(
            shaped((tiles, BLK, BLK), BF16),
            shaped((rows, BLK), F32),
            shaped((homes * IB_DEV, BLK), F32),
        ),
        in_specs=[SMEM] * owners + [VMEM] * (owners + 1 + owners + 2 * (homes - 1)),
        out_specs=(VMEM, VMEM, VMEM),
        scratch_shapes=[
            pltpu.SMEM((owners, homes), jnp.int32),
            pltpu.VMEM((rows * BLK, EMB), BF16),
            pltpu.VMEM((homes * IB_DEV * BLK, EMB), BF16),
            pltpu.VMEM((rows, BLK, BLK), F32),
            pltpu.VMEM((rows, BLK, BLK), F32),
            pltpu.VMEM((homes * IB_DEV, 8, BLK), F32),
        ],
        compiler_params=pltpu.CompilerParams(vmem_limit_bytes=LIMIT),
        name="first",
    )(*notes, *notes, imp, *adv, *mine, *theirs)


def run_next(owners, homes, last, notes, values, spans, parts, old, factors):
    tiles = owners * homes
    rows = owners * AB_DEV
    rounds = len(factors)
    price = shaped((homes * IB_DEV, BLK), F32)
    outs = (shaped((AB_DEV if last else rows, BLK), F32), price) + (() if last else (price,))
    return pl.pallas_call(
        functools.partial(next_kernel, owners, homes, rounds, last, spans),
        out_shape=outs,
        in_specs=[SMEM] * owners + [VMEM] * (owners + 1 + len(parts) + rounds - 1 + rounds),
        out_specs=(VMEM,) * len(outs),
        scratch_shapes=[
            pltpu.SMEM((owners, homes), jnp.int32),
            pltpu.VMEM((tiles, BLK, BLK), F32),
            pltpu.VMEM((rows, BLK, BLK), F32),
            pltpu.VMEM((rounds, rows, BLK, BLK), F32),
            pltpu.VMEM((rounds, homes * IB_DEV, BLK), F32),
            pltpu.VMEM((homes * IB_DEV, 8, BLK), F32),
        ],
        compiler_params=pltpu.CompilerParams(vmem_limit_bytes=LIMIT),
        name="last" if last else "middle",
    )(*notes, *notes, values, *parts, *old, *factors)


def swap_imp(x, mask, size):
    return lax.ppermute(x, "imp", [(i, i ^ mask) for i in range(size)])


def swap_core(x):
    return lax.ppermute(x, "adv", [(0, 1), (1, 0)])


def collect(x, masks, size):
    held = {0: x}
    high = [m for m in masks if m != 1]
    for pick in range(1, 1 << len(high)):
        d = functools.reduce(lambda a, j: a ^ (high[j] if pick >> j & 1 else 0), range(len(high)), 0)
        held[d] = swap_imp(x, d, size)
    if 1 in masks:
        for d in list(held):
            held[d ^ 1] = swap_imp(held[d], 1, size)
    return held


def swap_both(x, mask, size):
    perm = [(i * 2 + c, (i ^ mask) * 2 + 1 - c) for i in range(size) for c in range(2)]
    return lax.ppermute(x, ("imp", "adv"), perm)


def reorder(price, mask, homes):
    shape = (homes // (2 * mask), 2, mask * IB_DEV, BLK)
    return price.reshape(shape)[:, ::-1].reshape(price.shape)


def exchange(price, split, homes):
    for b in split[1:]:
        price = price + reorder(swap_imp(price, b, homes), b, homes)
    if not split:
        return (0, 0), [price, swap_core(price)]
    b = split[0]
    if JOIN:
        return (0, 0, b, b), [
            price,
            swap_core(price),
            swap_imp(price, b, homes),
            swap_both(price, b, homes),
        ]
    price = price + swap_core(price)
    return (0, b), [price, swap_imp(price, b, homes)]


def small_local(homes, imp_emb, adv_emb, allowances, eligible_slots):
    bits = [1 << b for b in range(homes.bit_length() - 1)]
    rep = [b for b in bits if b in REP_BITS]
    split = [b for b in bits if b not in REP_BITS]
    core = lax.axis_index("adv")
    half = lax.dynamic_slice_in_dim(imp_emb, core * BLK, BLK, 0)
    notes = jnp.concatenate(
        [allowances.reshape(AB_DEV, BLK), jnp.pad(eligible_slots, ((0, 0), (0, BLK - homes)))]
    )
    notes = collect(notes, rep, homes)
    halves = collect(half, bits, homes)
    adv = collect(adv_emb, rep, homes)
    order = sorted(adv)
    owners = len(order)
    mine = [halves[m] for m in range(1, homes)]
    theirs = [swap_core(h) for h in mine]
    notes = [notes[d] for d in order]
    values, factor, price = run_first(
        owners, homes, notes, imp_emb, [adv[d] for d in order], mine, theirs
    )
    old = []
    factors = [factor]
    for t in range(ITERS):
        last = t == ITERS - 1
        spans, parts = exchange(price, split, homes)
        outs = run_next(owners, homes, last, notes, values, spans, parts, old, factors)
        fresh, price = outs[:2]
        factors.append(fresh)
        old.extend(outs[2:])
    spans, parts = exchange(price, split, homes)
    terms = [x[d * IB_DEV : (d + 1) * IB_DEV] for d, x in zip(spans, parts)]
    while len(terms) > 1:
        terms = [terms[i] + terms[i + 1] for i in range(0, len(terms), 2)]
    return terms[0].reshape(IB_DEV * BLK), factors[-1].reshape(AB_DEV * BLK)


def large_local(imp_emb, adv_emb, allowances, eligible_slots):
    slot_count = eligible_slots.shape[1]
    adv_blocks = adv_emb.shape[0] // BLK
    slot_codes = eligible_slots[0]
    is_live = slot_codes >= 0
    clamped = jnp.maximum(slot_codes, 0)
    adv_pick = clamped // IB_DEV
    imp_pick = clamped % IB_DEV
    wanted = jnp.where(is_live, imp_pick, -1)
    cached = []

    def asked_blocks():
        if not cached:
            cached.append(lax.all_to_all(wanted, "imp", split_axis=0, concat_axis=0, tiled=True))
        return cached[0]

    adv_rows = jnp.take(adv_emb.reshape(adv_blocks, BLK, EMB), adv_pick, axis=0)
    score_scale = 1.0 / math.sqrt(EMB)
    asked = asked_blocks()
    home_slabs = imp_emb.reshape(IB_DEV, BLK, EMB)
    chosen = jnp.take(home_slabs, jnp.maximum(asked, 0), axis=0)
    outgoing = jnp.where((asked >= 0)[:, None, None], chosen, jnp.zeros_like(chosen))
    scores = (
        jnp.einsum(
            "nae,nbe->nab",
            adv_rows,
            lax.all_to_all(outgoing, "imp", split_axis=0, concat_axis=0, tiled=True),
            preferred_element_type=jnp.float32,
        )
        * score_scale
    )
    value_tiles = jnp.where(is_live[:, None, None], jax.nn.softplus(scores), 0.0).astype(
        jnp.bfloat16
    )
    highest = lax.Precision.HIGHEST
    spend_rows = allowances.astype(jnp.float32).reshape(adv_blocks, BLK) / 1024.0
    block_ids = jnp.arange(adv_blocks, dtype=jnp.int32)
    picker = (adv_pick[:, None] == block_ids[None, :]).astype(jnp.float32)
    live_picker = picker * is_live[:, None].astype(jnp.float32)
    row_totals = jnp.sum(value_tiles, axis=2, dtype=jnp.float32)
    value_sums = jnp.einsum("nk,na->ka", live_picker, row_totals, precision=highest)
    slot_spend = jnp.einsum("nk,ka->na", live_picker, spend_rows, precision=highest)
    slot_sums = jnp.einsum("nk,ka->na", picker, value_sums, precision=highest)
    bid_tiles = (slot_spend / slot_sums)[:, :, None] * value_tiles
    home_ids = jnp.arange(IB_DEV, dtype=jnp.int32)
    utility = jnp.zeros((adv_blocks, BLK), jnp.float32)
    home_prices = jnp.zeros((IB_DEV, BLK), jnp.float32)
    slot_prices = jnp.zeros((slot_count, BLK), jnp.float32)
    for round_index in range(ITERS + 1):
        totals = jnp.sum(bid_tiles, axis=1)
        asked = asked_blocks()
        asked_picker = (asked[:, None] == home_ids[None, :]).astype(jnp.float32)
        arrived = lax.all_to_all(totals, "imp", split_axis=0, concat_axis=0, tiled=True)
        partial_value = jnp.einsum("ok,oj->kj", asked_picker, arrived, precision=highest)
        home_prices = lax.psum(partial_value, "adv")
        if round_index < ITERS:
            returned = jnp.einsum("ok,kj->oj", asked_picker, home_prices, precision=highest)
            slot_prices = lax.all_to_all(returned, "imp", split_axis=0, concat_axis=0, tiled=True)
        if round_index < ITERS:
            divisor = jnp.where(is_live[:, None], slot_prices, 1.0)
            shares = bid_tiles / divisor[:, None, :]
            earned = value_tiles * shares
            utility = jnp.einsum(
                "nk,na->ka", live_picker, jnp.sum(earned, axis=2), precision=highest
            )
            slot_utility = jnp.einsum("nk,ka->na", picker, utility, precision=highest)
            bid_tiles = (slot_spend / slot_utility)[:, :, None] * earned
    return (home_prices.reshape(IB_DEV * BLK), utility.reshape(adv_blocks * BLK))


def solution(mesh):
    homes = mesh.shape["imp"]
    local = functools.partial(small_local, homes) if homes <= SMALL_IMP else large_local
    return jax.shard_map(
        local,
        mesh=mesh,
        in_specs=(
            P(("groups", "imp"), None),
            P(("groups", "imp", "adv"), None),
            P(("groups", "imp", "adv")),
            P(("groups", "imp", "adv"), None),
        ),
        out_specs=(P(("groups", "imp")), P(("groups", "imp", "adv"))),
        check_vma=False,
    )
```

```python
import functools
import math

import jax
import jax.numpy as jnp
from jax import lax
from jax.experimental import pallas as pl
from jax.experimental.pallas import tpu as pltpu
from jax.sharding import PartitionSpec as P

BLK = 128
EMB = 256
IB_DEV = 2
AB_DEV = 2
ITERS = 2
HOMES = 8
WIDE = IB_DEV * BLK
NOTES = 16
REP = (2, 4)
GROUPS = ((0, 2, 4, 6),)

F32 = jnp.float32
BF16 = jnp.bfloat16
SMEM = pl.BlockSpec(memory_space=pltpu.SMEM)
VMEM = pl.BlockSpec(memory_space=pltpu.VMEM)
LIMIT = 24 << 20


def take(refs, *counts):
    parts = []
    for n in counts:
        parts.append(refs[:n])
        refs = refs[n:]
    return (*parts, refs)


def make_eye():
    return lax.broadcasted_iota(jnp.int32, (BLK, BLK), 0) == lax.broadcasted_iota(
        jnp.int32, (BLK, BLK), 1
    )


def softplus(s):
    e = jnp.exp(-jnp.abs(s))
    near = e - (e * e) * (0.5 - e * (1.0 / 3.0))
    return jnp.maximum(s, 0.0) + jnp.where(e < 0.004, near, jnp.log(1.0 + e))


def fold(tile):
    return jnp.sum(tile.reshape(BLK // 8, 8, BLK), axis=0)


def slot_of(codes, owner, home):
    code = codes[owner][lax.bitwise_xor(lax.axis_index("imp"), home)]
    clamped = jnp.maximum(code, 0)
    return code >= 0, lax.shift_right_logical(clamped, 1), lax.bitwise_and(clamped, 1)


def row_block(ref, index):
    return ref[pl.ds(pl.multiple_of(index * BLK, BLK), BLK), :]


def gather_homes(imp_s, core, own, arrived):
    imp_s[pl.ds(0, WIDE), :] = own[...]
    for first, second, ref in arrived:
        d = jnp.where(core == 0, first, second)
        imp_s[pl.ds(pl.multiple_of(d * WIDE, WIDE), WIDE), :] = ref[...]


def score(lhs, rhs):
    return lax.dot_general(
        lhs, rhs, (((1,), (1,)), ((), ())), preferred_element_type=F32
    ) * (1.0 / math.sqrt(EMB))


def value_kernel(count, arrivals, *refs):
    own = arrivals is not None
    adv, refs = take(refs, count)
    eye = make_eye()
    if own:
        imp_own, *blocks = refs[: 1 + len(arrivals)]
        refs = refs[1 + len(arrivals) :]
        values, spend_out, factor_out, price_out, code_out, imp_s, table, sem, acc, pacc = refs
    else:
        imp_s, price_in, *refs = refs
        values, spend_out, factor_out, price_out, code_out, table, sem, acc, pacc = refs
    notes = [adv[o][pl.ds(WIDE, NOTES), :].astype(F32) for o in range(count)]
    for o in range(count):
        code_out[pl.ds(o, 1), :] = notes[o][2:3, :BLK].astype(jnp.int32)
    copy = pltpu.make_async_copy(code_out, table, sem)
    copy.start()
    if own:
        core = lax.axis_index("adv")
        gather_homes(imp_s, core, imp_own, [(*d, r) for d, r in zip(arrivals, blocks)])
        pacc[...] = jnp.zeros_like(pacc)
    else:
        for row in range(HOMES * IB_DEV):
            pacc[row] = jnp.concatenate(
                [price_in[pl.ds(row, 1), :], jnp.zeros((7, BLK), F32)], axis=0
            )
    for o in range(count):
        spending = (notes[o][0:1] * 128.0 + notes[o][1:2]) * (1.0 / 1024.0)
        for k in range(AB_DEV):
            row = spending[:, k * BLK : (k + 1) * BLK]
            col = jnp.sum(jnp.where(eye, row, 0.0), axis=1, keepdims=True)
            spend_out[o * AB_DEV + k] = jnp.broadcast_to(col, (BLK, BLK))
    copy.wait()
    codes = [table.at[o] for o in range(count)]
    acc[...] = jnp.zeros_like(acc)

    def value_body(m, carry):
        slots = [slot_of(codes, o, m) for o in range(count)]
        picked = [row_block(adv[o], slots[o][1]) for o in range(count)]
        if WIDE_DOT:
            rhs = imp_s[pl.ds(pl.multiple_of(m * WIDE, WIDE), WIDE), :]
            lhs = jnp.concatenate(picked, axis=0)
            both = score(lhs, rhs)
        for o, (live, k, b) in enumerate(slots):
            if WIDE_DOT:
                s = both[o * BLK : (o + 1) * BLK]
                s = jnp.where(b == 0, s[:, :BLK], s[:, BLK:])
            else:
                s = score(picked[o], row_block(imp_s, m * IB_DEV + b))
            v = jnp.where(live, softplus(s), 0.0).astype(BF16)
            values[o * HOMES + m] = v
            acc[o * AB_DEV + k] += v.astype(F32)
        return carry

    lax.fori_loop(0, HOMES, value_body, 0, unroll=max(1, UNROLL_V // count))
    for r in range(count * AB_DEV):
        total = jnp.sum(acc[r], axis=1, keepdims=True)
        factor_out[r] = spend_out[r] / total

    def bid_body(m, carry):
        for o in range(count):
            _, k, b = slot_of(codes, o, m)
            pacc[m * IB_DEV + b] += fold(
                factor_out[o * AB_DEV + k] * values[o * HOMES + m].astype(F32)
            )
        return carry

    lax.fori_loop(0, HOMES, bid_body, 0, unroll=max(1, UNROLL_B // count))
    for row in range(HOMES * IB_DEV):
        price_out[pl.ds(row, 1), :] = jnp.sum(pacc[row], axis=0, keepdims=True)


def add_prices(parts):
    rows = []
    for m in range(HOMES):
        terms = [ref[pl.ds((m ^ d) * IB_DEV, IB_DEV), :] for d, ref in parts]
        while len(terms) > 1:
            terms = [terms[i] + terms[i + 1] for i in range(0, len(terms), 2)]
        rows.append(terms[0])
    return jnp.concatenate(rows, axis=0)


def update_kernel(sizes, rounds, last, spans, *refs):
    owners, groups = sum(sizes), len(sizes)
    codes, values, spends, parts, old, firsts, factors, rest = take(
        refs, groups, groups, groups, len(spans), rounds - 1, groups, rounds - 1
    )
    place = [(g, o) for g, n in enumerate(sizes) for o in range(n)]
    codes = [codes[g].at[o] for g, o in place]
    if last:
        fresh_out, price_out, earned_s, acc, fac, rps, pacc = rest
    else:
        fresh_out, price_out, rps_out, earned_s, acc, fac, rps, pacc = rest
    full = add_prices(list(zip(spans, parts)))
    now = rounds - 1
    rps[now] = jnp.where(full > 0.0, 1.0 / full, 1.0)
    if not last:
        rps_out[...] = rps[now]
    for t in range(now):
        rps[t] = old[t][...]
    acc[...] = jnp.zeros_like(acc)
    pacc[...] = jnp.zeros_like(pacc)

    def earn_body(m, carry):
        for o in range(owners):
            g, at = place[o]
            _, k, b = slot_of(codes, o, m)
            v = values[g][at * HOMES + m].astype(F32)
            earned = v
            for t in range(rounds):
                factor = firsts[g][at * AB_DEV + k] if t == 0 else factors[t - 1][o * AB_DEV + k]
                earned = v * ((factor * earned) * rps[t, pl.ds(m * IB_DEV + b, 1), :])
            earned_s[o * HOMES + m] = earned
            acc[o * AB_DEV + k] += earned
        return carry

    lax.fori_loop(0, HOMES, earn_body, 0, unroll=UNROLL_E)
    for r in range(owners * AB_DEV):
        utility = jnp.sum(acc[r], axis=1, keepdims=True)
        g, at = place[r // AB_DEV]
        factor = spends[g][at * AB_DEV + r % AB_DEV] / utility
        fac[r] = factor
        if not last:
            fresh_out[r] = factor
        elif r < AB_DEV:
            fresh_out[pl.ds(r, 1), :] = jnp.sum(
                jnp.where(make_eye(), utility, 0.0), axis=0, keepdims=True
            )

    def bid_body(m, carry):
        for o in range(owners):
            _, k, b = slot_of(codes, o, m)
            pacc[m * IB_DEV + b] += fold(fac[o * AB_DEV + k] * earned_s[o * HOMES + m])
        return carry

    lax.fori_loop(0, HOMES, bid_body, 0, unroll=UNROLL_B)
    for row in range(HOMES * IB_DEV):
        price_out[pl.ds(row, 1), :] = jnp.sum(pacc[row], axis=0, keepdims=True)


UNROLL_V = 16
WIDE_DOT = False
JOIN = 2
UNROLL_B = 8
UNROLL_E = 2


def shaped(shape, dtype=F32):
    return jax.ShapeDtypeStruct(shape, dtype)


PRICE = (HOMES * IB_DEV, BLK)
PARTIAL = pltpu.VMEM((HOMES * IB_DEV, 8, BLK), F32)
GRANT = pltpu.CompilerParams(vmem_limit_bytes=LIMIT)


def run_values(adv, arrivals, last, *operands):
    own = arrivals is not None
    count = len(adv)
    columns = (count * AB_DEV, BLK, BLK)
    outs = [
        shaped((count * HOMES, BLK, BLK), BF16),
        shaped(columns),
        shaped(columns),
        shaped(PRICE),
        shaped((8, BLK), jnp.int32),
    ]
    homes = (HOMES * WIDE, EMB)
    scratch = [
        pltpu.SMEM((8, BLK), jnp.int32),
        pltpu.SemaphoreType.DMA,
        pltpu.VMEM(columns, F32),
        PARTIAL,
    ]
    if own and last:
        scratch.insert(0, pltpu.VMEM(homes, BF16))
    elif own:
        outs.append(shaped(homes, BF16))
    return pl.pallas_call(
        functools.partial(value_kernel, count, arrivals),
        out_shape=outs,
        in_specs=[VMEM] * (count + len(operands)),
        out_specs=[VMEM] * len(outs),
        scratch_shapes=scratch,
        compiler_params=GRANT,
        name="own_values" if own else "more_values",
    )(*adv, *operands)


def run_update(sizes, last, codes, values, spends, spans, parts, old, firsts, factors):
    owners = sum(sizes)
    rows = owners * AB_DEV
    rounds = len(factors) + 1
    outs = [shaped((AB_DEV, BLK) if last else (rows, BLK, BLK)), shaped(PRICE)]
    if not last:
        outs.append(shaped(PRICE))
    operands = [*values, *spends, *parts, *old, *firsts, *factors]
    return pl.pallas_call(
        functools.partial(update_kernel, sizes, rounds, last, spans),
        out_shape=outs,
        in_specs=[SMEM] * len(sizes) + [VMEM] * len(operands),
        out_specs=[VMEM] * len(outs),
        scratch_shapes=[
            pltpu.VMEM((owners * HOMES, BLK, BLK), F32),
            pltpu.VMEM((rows, BLK, BLK), F32),
            pltpu.VMEM((rows, BLK, BLK), F32),
            pltpu.VMEM((rounds, *PRICE), F32),
            PARTIAL,
        ],
        compiler_params=GRANT,
        name="last_update" if last else "update",
    )(*codes, *operands)


def move(x, *masks, cores=(0, 1), flip=0):
    if len(masks) == 1:
        masks = masks * 2
    perm = [
        (i * 2 + c, (i ^ masks[c]) * 2 + (c ^ flip)) for i in range(HOMES) for c in cores
    ]
    return lax.ppermute(x, ("imp", "adv"), perm)


def spread(x):
    held = {0: x}
    high = [m for m in REP if m != 1]
    for pick in range(1, 1 << len(high)):
        d = functools.reduce(lambda a, j: a ^ (high[j] if pick >> j & 1 else 0), range(len(high)), 0)
        held[d] = move(x, d)
    if 1 in REP:
        for d in list(held):
            held[d ^ 1] = move(held[d], 1)
    return held


def exchange(price, split):
    for b in split[1:]:
        shape = (HOMES // (2 * b), 2, b * IB_DEV, BLK)
        price = price + move(price, b).reshape(shape)[:, ::-1].reshape(PRICE)
    if not split:
        return (0, 0), [price, move(price, 0, flip=1)]
    b = split[0]
    if JOIN == 0:
        price = price + move(price, 0, flip=1)
        return (0, b), [price, move(price, b)]
    if JOIN == 1:
        shape = (HOMES // (2 * b), 2, b * IB_DEV, BLK)
        price = price + move(price, b).reshape(shape)[:, ::-1].reshape(PRICE)
        return (0, 0), [price, move(price, 0, flip=1)]
    here = [price, move(price, 0, flip=1)]
    there = [move(price, b), move(price, b, flip=1)]
    return (0, 0, b, b), here + there


def small_body(imp_emb, adv_emb, allowances, eligible_slots):
    split = [b for b in (1, 2, 4) if b not in REP]
    note = jnp.concatenate(
        [
            lax.shift_right_logical(allowances, 7).reshape(1, WIDE),
            lax.bitwise_and(allowances, 127).reshape(1, WIDE),
            jnp.pad(eligible_slots, ((0, 0), (0, WIDE - HOMES))),
            jnp.zeros((NOTES - 3, WIDE), jnp.int32),
        ]
    )
    adv = spread(jnp.concatenate([adv_emb, note.astype(BF16)]))
    near = move(imp_emb, 2, 4)
    far = move(imp_emb, 6, 1)
    near_x = move(near, 1)
    far_x = move(far, 1, cores=(0,))
    blocks = [
        near, move(near, 0, flip=1), far, move(far, 0, flip=1), near_x, move(near_x, 0, flip=1)
    ]
    tail = move(far_x, 0, cores=(0,), flip=1)
    arrivals = [(2, 4), (4, 2), (6, 1), (1, 6), (3, 5), (5, 3)]
    blocks.append(jnp.where(lax.axis_index("adv") == 0, far_x, tail))
    arrivals.append((7, 7))
    values, spends, firsts, codes, price, homes = [], [], [], [], None, None
    for group in GROUPS:
        first = homes is None
        v, sp, f, price, c, *rest = run_values(
            [adv[d] for d in group],
            tuple(arrivals) if first else None,
            group is GROUPS[-1],
            *((imp_emb, *blocks) if first else (homes, price)),
        )
        homes = rest[0] if rest else homes
        values.append(v)
        spends.append(sp)
        firsts.append(f)
        codes.append(c)
    sizes = tuple(len(group) for group in GROUPS)
    old, factors = [], []
    for t in range(ITERS):
        last = t == ITERS - 1
        spans, parts = exchange(price, split)
        fresh, price, *inverse = run_update(
            sizes, last, codes, values, spends, spans, parts, old, firsts, factors
        )
        factors.append(fresh)
        old.extend(inverse)
    spans, parts = exchange(price, split)
    terms = [x[d * IB_DEV : (d + 1) * IB_DEV] for d, x in zip(spans, parts)]
    while len(terms) > 1:
        terms = [terms[i] + terms[i + 1] for i in range(0, len(terms), 2)]
    return terms[0].reshape(IB_DEV * BLK), factors[-1].reshape(AB_DEV * BLK)


def small_local(*args):
    return small_body(*args)


def large_local(imp_emb, adv_emb, allowances, eligible_slots):
    slot_count = eligible_slots.shape[1]
    adv_blocks = adv_emb.shape[0] // BLK
    slot_codes = eligible_slots[0]
    is_live = slot_codes >= 0
    clamped = jnp.maximum(slot_codes, 0)
    adv_pick = clamped // IB_DEV
    imp_pick = clamped % IB_DEV
    wanted = jnp.where(is_live, imp_pick, -1)
    cached = []

    def asked_blocks():
        if not cached:
            cached.append(lax.all_to_all(wanted, "imp", split_axis=0, concat_axis=0, tiled=True))
        return cached[0]

    adv_rows = jnp.take(adv_emb.reshape(adv_blocks, BLK, EMB), adv_pick, axis=0)
    score_scale = 1.0 / math.sqrt(EMB)
    asked = asked_blocks()
    home_slabs = imp_emb.reshape(IB_DEV, BLK, EMB)
    chosen = jnp.take(home_slabs, jnp.maximum(asked, 0), axis=0)
    outgoing = jnp.where((asked >= 0)[:, None, None], chosen, jnp.zeros_like(chosen))
    scores = (
        jnp.einsum(
            "nae,nbe->nab",
            adv_rows,
            lax.all_to_all(outgoing, "imp", split_axis=0, concat_axis=0, tiled=True),
            preferred_element_type=jnp.float32,
        )
        * score_scale
    )
    value_tiles = jnp.where(is_live[:, None, None], jax.nn.softplus(scores), 0.0).astype(
        jnp.bfloat16
    )
    highest = lax.Precision.HIGHEST
    spend_rows = allowances.astype(jnp.float32).reshape(adv_blocks, BLK) / 1024.0
    block_ids = jnp.arange(adv_blocks, dtype=jnp.int32)
    picker = (adv_pick[:, None] == block_ids[None, :]).astype(jnp.float32)
    live_picker = picker * is_live[:, None].astype(jnp.float32)
    row_totals = jnp.sum(value_tiles, axis=2, dtype=jnp.float32)
    value_sums = jnp.einsum("nk,na->ka", live_picker, row_totals, precision=highest)
    slot_spend = jnp.einsum("nk,ka->na", live_picker, spend_rows, precision=highest)
    slot_sums = jnp.einsum("nk,ka->na", picker, value_sums, precision=highest)
    bid_tiles = (slot_spend / slot_sums)[:, :, None] * value_tiles
    home_ids = jnp.arange(IB_DEV, dtype=jnp.int32)
    utility = jnp.zeros((adv_blocks, BLK), jnp.float32)
    home_prices = jnp.zeros((IB_DEV, BLK), jnp.float32)
    slot_prices = jnp.zeros((slot_count, BLK), jnp.float32)
    for round_index in range(ITERS + 1):
        totals = jnp.sum(bid_tiles, axis=1)
        asked = asked_blocks()
        asked_picker = (asked[:, None] == home_ids[None, :]).astype(jnp.float32)
        arrived = lax.all_to_all(totals, "imp", split_axis=0, concat_axis=0, tiled=True)
        partial_value = jnp.einsum("ok,oj->kj", asked_picker, arrived, precision=highest)
        home_prices = lax.psum(partial_value, "adv")
        if round_index < ITERS:
            returned = jnp.einsum("ok,kj->oj", asked_picker, home_prices, precision=highest)
            slot_prices = lax.all_to_all(returned, "imp", split_axis=0, concat_axis=0, tiled=True)
        if round_index < ITERS:
            divisor = jnp.where(is_live[:, None], slot_prices, 1.0)
            shares = bid_tiles / divisor[:, None, :]
            earned = value_tiles * shares
            utility = jnp.einsum(
                "nk,na->ka", live_picker, jnp.sum(earned, axis=2), precision=highest
            )
            slot_utility = jnp.einsum("nk,ka->na", picker, utility, precision=highest)
            bid_tiles = (slot_spend / slot_utility)[:, :, None] * earned
    return (home_prices.reshape(IB_DEV * BLK), utility.reshape(adv_blocks * BLK))


def solution(mesh):
    small = mesh.shape["imp"] == HOMES and mesh.shape["adv"] == 2
    return jax.shard_map(
        small_local if small else large_local,
        mesh=mesh,
        in_specs=(
            P(("groups", "imp"), None),
            P(("groups", "imp", "adv"), None),
            P(("groups", "imp", "adv")),
            P(("groups", "imp", "adv"), None),
        ),
        out_specs=(P(("groups", "imp")), P(("groups", "imp", "adv"))),
        check_vma=False,
    )
```

```python
import functools
import math

import jax
import jax.numpy as jnp
from jax import lax
from jax.experimental import pallas as pl
from jax.experimental.pallas import tpu as pltpu
from jax.sharding import PartitionSpec as P

BLK = 128
EMB = 256
IB_DEV = 2
AB_DEV = 2
ITERS = 2
HOMES = 8
WIDE = IB_DEV * BLK
NOTES = 16
REP = (2, 4)
GROUPS = ((0, 2, 4, 6),)

F32 = jnp.float32
BF16 = jnp.bfloat16
SMEM = pl.BlockSpec(memory_space=pltpu.SMEM)
VMEM = pl.BlockSpec(memory_space=pltpu.VMEM)
LIMIT = 12 << 20


def take(refs, *counts):
    parts = []
    for n in counts:
        parts.append(refs[:n])
        refs = refs[n:]
    return (*parts, refs)


def make_eye():
    return lax.broadcasted_iota(jnp.int32, (BLK, BLK), 0) == lax.broadcasted_iota(
        jnp.int32, (BLK, BLK), 1
    )


def softplus(s):
    e = jnp.exp(-jnp.abs(s))
    near = e - (0.5 * e) * e
    return jnp.maximum(s, 0.0) + jnp.where(e < 0.001, near, jnp.log(1.0 + e))


def fold(tile):
    return jnp.sum(tile.reshape(BLK // 8, 8, BLK), axis=0)


def slot_of(codes, home, owner, owners):
    code = codes[lax.bitwise_xor(lax.axis_index("imp"), home)]
    clamped = jnp.maximum(code, 0)
    k, b = lax.shift_right_logical(clamped, 1), lax.bitwise_and(clamped, 1)
    live = code >= 0
    row = jnp.where(live, owner * AB_DEV + k, owners * AB_DEV)
    return k, b, row, jnp.where(live, home * IB_DEV + b, HOMES * IB_DEV)


def row_block(ref, index):
    return ref[pl.ds(pl.multiple_of(index * BLK, BLK), BLK), :]


def gather_homes(imp_s, core, own, arrived):
    imp_s[pl.ds(0, WIDE), :] = own[...]
    for first, second, ref in arrived:
        d = jnp.where(core == 0, first, second)
        imp_s[pl.ds(pl.multiple_of(d * WIDE, WIDE), WIDE), :] = ref[...]


def pack_kernel(adv, allow, slots, imp, adv_out, imp_out, allow_s, slots_s, sems):
    moves = [
        pltpu.make_async_copy(allow, allow_s, sems.at[0]),
        pltpu.make_async_copy(slots, slots_s, sems.at[1]),
        pltpu.make_async_copy(adv, adv_out.at[pl.ds(0, WIDE), :], sems.at[2]),
        pltpu.make_async_copy(imp, imp_out, sems.at[3]),
    ]
    for move in moves:
        move.start()
    for move in moves[:2]:
        move.wait()
    spend = allow_s[...].reshape(1, WIDE)
    codes = jnp.concatenate([slots_s[...], jnp.zeros((1, WIDE - HOMES), jnp.int32)], axis=1)
    rows = [
        lax.shift_right_logical(spend, 7),
        lax.bitwise_and(spend, 127),
        codes,
        jnp.zeros((NOTES - 3, WIDE), jnp.int32),
    ]
    note = jnp.concatenate(rows, axis=0).astype(F32).astype(BF16)
    adv_out[pl.ds(WIDE, NOTES), :] = note
    for move in moves[2:]:
        move.wait()


def score(lhs, rhs):
    return lax.dot_general(
        lhs, rhs, (((1,), (1,)), ((), ())), preferred_element_type=F32
    ) * (1.0 / math.sqrt(EMB))


def value_kernel(count, arrivals, *refs):
    own = arrivals is not None
    adv, refs = take(refs, count)
    eye = make_eye()
    if own:
        imp_own, *blocks = refs[: 1 + len(arrivals)]
        refs = refs[1 + len(arrivals) :]
        values, spend_out, factor_out, price_out, code_out, imp_s, table, sem, acc, pacc = refs
    else:
        imp_s, price_in, *refs = refs
        values, spend_out, factor_out, price_out, code_out, table, sem, acc, pacc = refs
    notes = [adv[o][pl.ds(WIDE, NOTES), :].astype(F32) for o in range(count)]
    for o in range(count):
        code_out[pl.ds(o, 1), :] = notes[o][2:3, :BLK].astype(jnp.int32)
    copy = pltpu.make_async_copy(code_out, table, sem)
    copy.start()
    if own:
        core = lax.axis_index("adv")
        gather_homes(imp_s, core, imp_own, [(*d, r) for d, r in zip(arrivals, blocks)])
        pacc[...] = jnp.zeros_like(pacc)
    else:
        for row in range(HOMES * IB_DEV):
            pacc[row] = jnp.concatenate(
                [price_in[pl.ds(row, 1), :], jnp.zeros((7, BLK), F32)], axis=0
            )
    for o in range(count):
        spending = (notes[o][0:1] * 128.0 + notes[o][1:2]) * (1.0 / 1024.0)
        for k in range(AB_DEV):
            row = spending[:, k * BLK : (k + 1) * BLK]
            col = jnp.sum(jnp.where(eye, row, 0.0), axis=1, keepdims=True)
            spend_out[o * AB_DEV + k] = jnp.broadcast_to(col, (BLK, BLK))
    copy.wait()
    codes = [table.at[o] for o in range(count)]
    acc[...] = jnp.zeros_like(acc)

    def value_body(m, carry):
        for o in range(count):
            k, b, row, _ = slot_of(codes[o], m, o, count)
            s = score(row_block(adv[o], k), row_block(imp_s, m * IB_DEV + b))
            v = softplus(s).astype(BF16).astype(F32)
            values[o * HOMES + m] = v
            acc[row] += v
        return carry

    lax.fori_loop(0, HOMES, value_body, 0, unroll=max(1, UNROLL_V // count))
    for r in range(count * AB_DEV):
        total = jnp.sum(acc[r], axis=1, keepdims=True)
        factor_out[r] = spend_out[r] / total

    def bid_body(m, carry):
        for o in range(count):
            k, _, _, row = slot_of(codes[o], m, o, count)
            pacc[row] += fold(factor_out[o * AB_DEV + k] * values[o * HOMES + m])
        return carry

    lax.fori_loop(0, HOMES, bid_body, 0, unroll=max(1, UNROLL_B // count))
    for row in range(HOMES * IB_DEV):
        price_out[pl.ds(row, 1), :] = jnp.sum(pacc[row], axis=0, keepdims=True)


def add_prices(parts):
    rows = []
    for m in range(HOMES):
        terms = [ref[pl.ds((m ^ d) * IB_DEV, IB_DEV), :] for d, ref in parts]
        while len(terms) > 1:
            terms = [terms[i] + terms[i + 1] for i in range(0, len(terms), 2)]
        rows.append(terms[0])
    return jnp.concatenate(rows, axis=0)


def update_kernel(sizes, last, spans, *refs):
    owners, groups = sum(sizes), len(sizes)
    codes, values, spends, parts, refs = take(refs, groups, groups, groups, len(spans))
    place = [(g, o) for g, n in enumerate(sizes) for o in range(n)]
    codes = [codes[g].at[o] for g, o in place]
    if last:
        before, factors, utility_out, price_out, earned_s, acc, fac, rps, pacc = refs
    else:
        firsts, refs = take(refs, groups)
        fac, price_out, earned_s, acc, rps, pacc = refs
    full = add_prices(list(zip(spans, parts)))
    rps[...] = jnp.where(full > 0.0, 1.0 / full, 1.0)
    acc[...] = jnp.zeros_like(acc)
    pacc[...] = jnp.zeros_like(pacc)

    def earn_body(m, carry):
        for o, (g, at) in enumerate(place):
            k, b, row, _ = slot_of(codes[o], m, o, owners)
            v = values[g][at * HOMES + m]
            if last:
                bid = factors[o * AB_DEV + k] * before[o * HOMES + m]
            else:
                bid = firsts[g][at * AB_DEV + k] * v
            earned = v * (bid * rps[pl.ds(m * IB_DEV + b, 1), :])
            earned_s[o * HOMES + m] = earned
            acc[row] += earned
        return carry

    lax.fori_loop(0, HOMES, earn_body, 0, unroll=max(1, UNROLL_E // owners))
    for r in range(owners * AB_DEV):
        g, at = place[r // AB_DEV]
        utility = jnp.sum(acc[r], axis=1, keepdims=True)
        fac[r] = spends[g][at * AB_DEV + r % AB_DEV] / utility
        if last and r < AB_DEV:
            utility_out[r] = fold(jnp.where(make_eye(), utility, 0.0))

    def bid_body(m, carry):
        for o in range(owners):
            k, _, _, row = slot_of(codes[o], m, o, owners)
            pacc[row] += fold(fac[o * AB_DEV + k] * earned_s[o * HOMES + m])
        return carry

    lax.fori_loop(0, HOMES, bid_body, 0, unroll=max(1, UNROLL_P // owners))
    for row in range(HOMES * IB_DEV):
        price_out[pl.ds(row, 1), :] = jnp.sum(pacc[row], axis=0, keepdims=True)


UNROLL_P = 16
UNROLL_V = 16
JOIN = 2
UNROLL_B = 16
UNROLL_E = 16


def shaped(shape, dtype=F32):
    return jax.ShapeDtypeStruct(shape, dtype)


PRICE = (HOMES * IB_DEV, BLK)
PARTIAL = pltpu.VMEM((HOMES * IB_DEV + 1, 8, BLK), F32)
GRANT = pltpu.CompilerParams(vmem_limit_bytes=LIMIT)


def run_pack(*operands):
    operands = [pltpu.with_memory_space_constraint(x, pltpu.HBM) for x in operands]
    return pl.pallas_call(
        pack_kernel,
        out_shape=[shaped((WIDE + NOTES, EMB), BF16), shaped((WIDE, EMB), BF16)],
        in_specs=[pl.BlockSpec(memory_space=pltpu.HBM)] * 4,
        out_specs=[VMEM] * 2,
        scratch_shapes=[
            pltpu.VMEM((WIDE,), jnp.int32),
            pltpu.VMEM((1, HOMES), jnp.int32),
            pltpu.SemaphoreType.DMA((4,)),
        ],
        compiler_params=GRANT,
        name="pack",
    )(*operands)


def run_values(adv, arrivals, last, *operands):
    own = arrivals is not None
    count = len(adv)
    columns = (count * AB_DEV, BLK, BLK)
    outs = [
        shaped((count * HOMES, BLK, BLK)),
        shaped(columns),
        shaped(columns),
        shaped(PRICE),
        shaped((8, BLK), jnp.int32),
    ]
    homes = (HOMES * WIDE, EMB)
    scratch = [
        pltpu.SMEM((8, BLK), jnp.int32),
        pltpu.SemaphoreType.DMA,
        pltpu.VMEM((count * AB_DEV + 1, BLK, BLK), F32),
        PARTIAL,
    ]
    if own and last:
        scratch.insert(0, pltpu.VMEM(homes, BF16))
    elif own:
        outs.append(shaped(homes, BF16))
    return pl.pallas_call(
        functools.partial(value_kernel, count, arrivals),
        out_shape=outs,
        in_specs=[VMEM] * (count + len(operands)),
        out_specs=[VMEM] * len(outs),
        scratch_shapes=scratch,
        compiler_params=GRANT,
    )(*adv, *operands)


def run_update(sizes, last, codes, values, spends, spans, parts, before):
    owners = sum(sizes)
    rows = owners * AB_DEV
    columns = (rows, BLK, BLK)
    tiles = (owners * HOMES, BLK, BLK)
    if last:
        outs = [shaped((AB_DEV, 8, BLK)), shaped(PRICE)]
        scratch = [pltpu.VMEM(tiles, F32)]
        extra = [pltpu.VMEM(columns, F32)]
    else:
        outs = [shaped(columns), shaped(PRICE), shaped(tiles)]
        scratch = extra = []
    operands = [*values, *spends, *parts, *before]
    return pl.pallas_call(
        functools.partial(update_kernel, sizes, last, spans),
        out_shape=outs,
        in_specs=[SMEM] * len(sizes) + [VMEM] * len(operands),
        out_specs=[VMEM] * len(outs),
        scratch_shapes=[
            *scratch,
            pltpu.VMEM((rows + 1, BLK, BLK), F32),
            *extra,
            pltpu.VMEM(PRICE, F32),
            PARTIAL,
        ],
        compiler_params=GRANT,
        name="last_update" if last else "update",
    )(*codes, *operands)


def move(x, *masks, cores=(0, 1), flip=0):
    if len(masks) == 1:
        masks = masks * 2
    perm = [
        (i * 2 + c, (i ^ masks[c]) * 2 + (c ^ flip)) for i in range(HOMES) for c in cores
    ]
    return lax.ppermute(x, ("imp", "adv"), perm)


def spread(x):
    held = {0: x}
    high = [m for m in REP if m != 1]
    for pick in range(1, 1 << len(high)):
        d = functools.reduce(lambda a, j: a ^ (high[j] if pick >> j & 1 else 0), range(len(high)), 0)
        held[d] = move(x, d)
    if 1 in REP:
        for d in list(held):
            held[d ^ 1] = move(held[d], 1)
    return held


def exchange(price, split):
    for b in split[1:]:
        shape = (HOMES // (2 * b), 2, b * IB_DEV, BLK)
        price = price + move(price, b).reshape(shape)[:, ::-1].reshape(PRICE)
    if not split:
        return (0, 0), [price, move(price, 0, flip=1)]
    b = split[0]
    if JOIN == 0:
        price = price + move(price, 0, flip=1)
        return (0, b), [price, move(price, b)]
    if JOIN == 1:
        shape = (HOMES // (2 * b), 2, b * IB_DEV, BLK)
        price = price + move(price, b).reshape(shape)[:, ::-1].reshape(PRICE)
        return (0, 0), [price, move(price, 0, flip=1)]
    here = [price, move(price, 0, flip=1)]
    there = [move(price, b), move(price, b, flip=1)]
    return (0, 0, b, b), here + there


def small_body(imp_emb, adv_emb, allowances, eligible_slots):
    split = [b for b in (1, 2, 4) if b not in REP]
    packed, imp_own = run_pack(adv_emb, allowances, eligible_slots, imp_emb)
    adv = spread(packed)
    near = move(imp_emb, 2, 4)
    far = move(imp_emb, 6, 1)
    near_x = move(near, 1)
    far_x = move(far, 1, cores=(0,))
    blocks = [
        near, move(near, 0, flip=1), far, move(far, 0, flip=1), near_x, move(near_x, 0, flip=1)
    ]
    tail = move(far_x, 0, cores=(0,), flip=1)
    arrivals = [(2, 4), (4, 2), (6, 1), (1, 6), (3, 5), (5, 3)]
    blocks.append(jnp.where(lax.axis_index("adv") == 0, far_x, tail))
    arrivals.append((7, 7))
    values, spends, firsts, codes, price, homes = [], [], [], [], None, None
    for group in GROUPS:
        first = homes is None
        v, sp, f, price, c, *rest = run_values(
            [adv[d] for d in group],
            tuple(arrivals) if first else None,
            group is GROUPS[-1],
            *((imp_own, *blocks) if first else (homes, price)),
        )
        homes = rest[0] if rest else homes
        values.append(v)
        spends.append(sp)
        firsts.append(f)
        codes.append(c)
    sizes = tuple(len(group) for group in GROUPS)
    before = firsts
    for t in range(ITERS):
        last = t == ITERS - 1
        spans, parts = exchange(price, split)
        fresh, price, *earned = run_update(
            sizes, last, codes, values, spends, spans, parts, before
        )
        before = [*earned, fresh]
    utility = jnp.sum(fresh, axis=1)
    spans, parts = exchange(price, split)
    terms = [x[d * IB_DEV : (d + 1) * IB_DEV] for d, x in zip(spans, parts)]
    while len(terms) > 1:
        terms = [terms[i] + terms[i + 1] for i in range(0, len(terms), 2)]
    return terms[0].reshape(IB_DEV * BLK), utility.reshape(AB_DEV * BLK)


def small_local(*args):
    return small_body(*args)


def large_local(imp_emb, adv_emb, allowances, eligible_slots):
    slot_count = eligible_slots.shape[1]
    adv_blocks = adv_emb.shape[0] // BLK
    slot_codes = eligible_slots[0]
    is_live = slot_codes >= 0
    clamped = jnp.maximum(slot_codes, 0)
    adv_pick = clamped // IB_DEV
    imp_pick = clamped % IB_DEV
    wanted = jnp.where(is_live, imp_pick, -1)
    cached = []

    def asked_blocks():
        if not cached:
            cached.append(lax.all_to_all(wanted, "imp", split_axis=0, concat_axis=0, tiled=True))
        return cached[0]

    adv_rows = jnp.take(adv_emb.reshape(adv_blocks, BLK, EMB), adv_pick, axis=0)
    score_scale = 1.0 / math.sqrt(EMB)
    asked = asked_blocks()
    home_slabs = imp_emb.reshape(IB_DEV, BLK, EMB)
    chosen = jnp.take(home_slabs, jnp.maximum(asked, 0), axis=0)
    outgoing = jnp.where((asked >= 0)[:, None, None], chosen, jnp.zeros_like(chosen))
    scores = (
        jnp.einsum(
            "nae,nbe->nab",
            adv_rows,
            lax.all_to_all(outgoing, "imp", split_axis=0, concat_axis=0, tiled=True),
            preferred_element_type=jnp.float32,
        )
        * score_scale
    )
    value_tiles = jnp.where(is_live[:, None, None], jax.nn.softplus(scores), 0.0).astype(
        jnp.bfloat16
    )
    highest = lax.Precision.HIGHEST
    spend_rows = allowances.astype(jnp.float32).reshape(adv_blocks, BLK) / 1024.0
    block_ids = jnp.arange(adv_blocks, dtype=jnp.int32)
    picker = (adv_pick[:, None] == block_ids[None, :]).astype(jnp.float32)
    live_picker = picker * is_live[:, None].astype(jnp.float32)
    row_totals = jnp.sum(value_tiles, axis=2, dtype=jnp.float32)
    value_sums = jnp.einsum("nk,na->ka", live_picker, row_totals, precision=highest)
    slot_spend = jnp.einsum("nk,ka->na", live_picker, spend_rows, precision=highest)
    slot_sums = jnp.einsum("nk,ka->na", picker, value_sums, precision=highest)
    bid_tiles = (slot_spend / slot_sums)[:, :, None] * value_tiles
    home_ids = jnp.arange(IB_DEV, dtype=jnp.int32)
    utility = jnp.zeros((adv_blocks, BLK), jnp.float32)
    home_prices = jnp.zeros((IB_DEV, BLK), jnp.float32)
    slot_prices = jnp.zeros((slot_count, BLK), jnp.float32)
    for round_index in range(ITERS + 1):
        totals = jnp.sum(bid_tiles, axis=1)
        asked = asked_blocks()
        asked_picker = (asked[:, None] == home_ids[None, :]).astype(jnp.float32)
        arrived = lax.all_to_all(totals, "imp", split_axis=0, concat_axis=0, tiled=True)
        partial_value = jnp.einsum("ok,oj->kj", asked_picker, arrived, precision=highest)
        home_prices = lax.psum(partial_value, "adv")
        if round_index < ITERS:
            returned = jnp.einsum("ok,kj->oj", asked_picker, home_prices, precision=highest)
            slot_prices = lax.all_to_all(returned, "imp", split_axis=0, concat_axis=0, tiled=True)
        if round_index < ITERS:
            divisor = jnp.where(is_live[:, None], slot_prices, 1.0)
            shares = bid_tiles / divisor[:, None, :]
            earned = value_tiles * shares
            utility = jnp.einsum(
                "nk,na->ka", live_picker, jnp.sum(earned, axis=2), precision=highest
            )
            slot_utility = jnp.einsum("nk,ka->na", picker, utility, precision=highest)
            bid_tiles = (slot_spend / slot_utility)[:, :, None] * earned
    return (home_prices.reshape(IB_DEV * BLK), utility.reshape(adv_blocks * BLK))


def solution(mesh):
    small = mesh.shape["imp"] == HOMES and mesh.shape["adv"] == 2
    return jax.shard_map(
        small_local if small else large_local,
        mesh=mesh,
        in_specs=(
            P(("groups", "imp"), None),
            P(("groups", "imp", "adv"), None),
            P(("groups", "imp", "adv")),
            P(("groups", "imp", "adv"), None),
        ),
        out_specs=(P(("groups", "imp")), P(("groups", "imp", "adv"))),
        check_vma=False,
    )
```

```python
import functools
import math

import jax
import jax.numpy as jnp
from jax import lax
from jax.experimental import pallas as pl
from jax.experimental.pallas import tpu as pltpu
from jax.sharding import PartitionSpec as P

BLK = 128
EMB = 256
IB_DEV = 2
AB_DEV = 2
ITERS = 2
HOMES = 8
WIDE = IB_DEV * BLK
NOTES = 16
REP = (2, 4)
GROUPS = ((0, 2, 4, 6),)

F32 = jnp.float32
BF16 = jnp.bfloat16
SMEM = pl.BlockSpec(memory_space=pltpu.SMEM)
VMEM = pl.BlockSpec(memory_space=pltpu.VMEM)
LIMIT = 12 << 20


def take(refs, *counts):
    parts = []
    for n in counts:
        parts.append(refs[:n])
        refs = refs[n:]
    return (*parts, refs)


def make_eye():
    return lax.broadcasted_iota(jnp.int32, (BLK, BLK), 0) == lax.broadcasted_iota(
        jnp.int32, (BLK, BLK), 1
    )


def softplus(dot):
    scale = 1.0 / math.sqrt(EMB)
    s = dot * scale
    if FOLDED:
        e = jnp.exp2(jnp.abs(dot) * (-scale / math.log(2.0)))
    else:
        e = jnp.exp(-jnp.abs(s))
    near = e - (0.5 * e) * e
    return jnp.maximum(s, 0.0) + jnp.where(e < 0.001, near, jnp.log(1.0 + e))


def fold(tile):
    return jnp.sum(tile.reshape(BLK // 8, 8, BLK), axis=0)


def slot_of(codes, home, owner, owners):
    code = codes[lax.bitwise_xor(lax.axis_index("imp"), home)]
    clamped = jnp.maximum(code, 0)
    k, b = lax.shift_right_logical(clamped, 1), lax.bitwise_and(clamped, 1)
    live = code >= 0
    row = jnp.where(live, owner * AB_DEV + k, owners * AB_DEV)
    return k, b, row, jnp.where(live, home * IB_DEV + b, HOMES * IB_DEV)


def row_block(ref, index):
    return ref[pl.ds(pl.multiple_of(index * BLK, BLK), BLK), :]


def gather_homes(imp_s, core, own, arrived):
    imp_s[pl.ds(0, WIDE), :] = own[...]
    for first, second, ref in arrived:
        d = jnp.where(core == 0, first, second)
        imp_s[pl.ds(pl.multiple_of(d * WIDE, WIDE), WIDE), :] = ref[...]


def pack_kernel(adv, allow, slots, imp, adv_out, imp_out, allow_s, slots_s, sems):
    moves = [
        pltpu.make_async_copy(allow, allow_s, sems.at[0]),
        pltpu.make_async_copy(slots, slots_s, sems.at[1]),
        pltpu.make_async_copy(adv, adv_out.at[pl.ds(0, WIDE), :], sems.at[2]),
        pltpu.make_async_copy(imp, imp_out, sems.at[3]),
    ]
    for move in moves:
        move.start()
    for move in moves[:2]:
        move.wait()
    spend = allow_s[...].reshape(1, WIDE)
    codes = jnp.concatenate([slots_s[...], jnp.zeros((1, WIDE - HOMES), jnp.int32)], axis=1)
    rows = [
        lax.shift_right_logical(spend, 7),
        lax.bitwise_and(spend, 127),
        codes,
        jnp.zeros((NOTES - 3, WIDE), jnp.int32),
    ]
    note = jnp.concatenate(rows, axis=0).astype(F32).astype(BF16)
    adv_out[pl.ds(WIDE, NOTES), :] = note
    for move in moves[2:]:
        move.wait()


def score(lhs, rhs):
    return lax.dot_general(lhs, rhs, (((1,), (1,)), ((), ())), preferred_element_type=F32)


def value_kernel(count, arrivals, *refs):
    own = arrivals is not None
    adv, refs = take(refs, count)
    eye = make_eye()
    if own:
        imp_own, *blocks = refs[: 1 + len(arrivals)]
        refs = refs[1 + len(arrivals) :]
        values, spend_out, factor_out, price_out, code_out, imp_s, table, sem, acc, pacc = refs
    else:
        imp_s, price_in, *refs = refs
        values, spend_out, factor_out, price_out, code_out, table, sem, acc, pacc = refs
    notes = [adv[o][pl.ds(WIDE, NOTES), :].astype(F32) for o in range(count)]
    for o in range(count):
        code_out[pl.ds(o, 1), :] = notes[o][2:3, :BLK].astype(jnp.int32)
    copy = pltpu.make_async_copy(code_out, table, sem)
    copy.start()
    if own:
        core = lax.axis_index("adv")
        gather_homes(imp_s, core, imp_own, [(*d, r) for d, r in zip(arrivals, blocks)])
        pacc[...] = jnp.zeros_like(pacc)
    else:
        for row in range(HOMES * IB_DEV):
            pacc[row] = jnp.concatenate(
                [price_in[pl.ds(row, 1), :], jnp.zeros((7, BLK), F32)], axis=0
            )
    for o in range(count):
        spending = (notes[o][0:1] * 128.0 + notes[o][1:2]) * (1.0 / 1024.0)
        for k in range(AB_DEV):
            row = spending[:, k * BLK : (k + 1) * BLK]
            col = jnp.sum(jnp.where(eye, row, 0.0), axis=1, keepdims=True)
            spend_out[o * AB_DEV + k] = jnp.broadcast_to(col, (BLK, BLK))
    copy.wait()
    codes = [table.at[o] for o in range(count)]
    acc[...] = jnp.zeros_like(acc)

    def value_body(m, carry):
        for o in range(count):
            k, b, row, _ = slot_of(codes[o], m, o, count)
            s = score(row_block(adv[o], k), row_block(imp_s, m * IB_DEV + b))
            v = softplus(s).astype(BF16).astype(F32)
            values[o * HOMES + m] = v
            acc[row] += v
        return carry

    lax.fori_loop(0, HOMES, value_body, 0, unroll=max(1, UNROLL_V // count))
    for r in range(count * AB_DEV):
        total = jnp.sum(acc[r], axis=1, keepdims=True)
        factor_out[r] = spend_out[r] / total

    def bid_body(m, carry):
        for o in range(count):
            k, _, _, row = slot_of(codes[o], m, o, count)
            pacc[row] += fold(factor_out[o * AB_DEV + k] * values[o * HOMES + m])
        return carry

    lax.fori_loop(0, HOMES, bid_body, 0, unroll=max(1, UNROLL_B // count))
    for row in range(HOMES * IB_DEV):
        price_out[pl.ds(row, 1), :] = jnp.sum(pacc[row], axis=0, keepdims=True)


def add_prices(parts):
    rows = []
    for m in range(HOMES):
        terms = [ref[pl.ds((m ^ d) * IB_DEV, IB_DEV), :] for d, ref in parts]
        while len(terms) > 1:
            terms = [terms[i] + terms[i + 1] for i in range(0, len(terms), 2)]
        rows.append(terms[0])
    return jnp.concatenate(rows, axis=0)


def update_kernel(sizes, last, spans, wanted, *refs):
    owners, groups = sum(sizes), len(sizes)
    codes, values, spends, parts, refs = take(refs, groups, groups, groups, len(spans))
    place = [(g, o) for g, n in enumerate(sizes) for o in range(n)]
    codes = [codes[g].at[o] for g, o in place]
    if last:
        before, factors, utility_out, price_out, earned_s, acc, fac, rps, pacc = refs
    else:
        firsts, refs = take(refs, groups)
        fac, price_out, earned_s, acc, rps, pacc = refs
    full = add_prices(list(zip(spans, parts)))
    rps[...] = jnp.where(full > 0.0, 1.0 / full, 1.0)
    acc[...] = jnp.zeros_like(acc)
    pacc[...] = jnp.zeros_like(pacc)

    def earn_body(m, carry):
        for o, (g, at) in enumerate(place):
            k, b, row, _ = slot_of(codes[o], m, o, owners)
            v = values[g][at * HOMES + m]
            if last:
                bid = factors[o * AB_DEV + k] * before[o * HOMES + m]
            else:
                bid = firsts[g][at * AB_DEV + k] * v
            earned = v * (bid * rps[pl.ds(m * IB_DEV + b, 1), :])
            earned_s[o * HOMES + m] = earned
            acc[row] += earned
        return carry

    lax.fori_loop(0, HOMES, earn_body, 0, unroll=max(1, UNROLL_E // owners))
    for r in range(owners * AB_DEV):
        g, at = place[r // AB_DEV]
        utility = jnp.sum(acc[r], axis=1, keepdims=True)
        fac[r] = spends[g][at * AB_DEV + r % AB_DEV] / utility
        if last and r < AB_DEV:
            utility_out[r] = fold(jnp.where(make_eye(), utility, 0.0))

    def bid_body(m, carry):
        for o in range(owners):
            k, _, _, row = slot_of(codes[o], m, o, owners)
            pacc[row] += fold(fac[o * AB_DEV + k] * earned_s[o * HOMES + m])
        return carry

    if last:
        for m in wanted:
            bid_body(m, 0)
    else:
        lax.fori_loop(0, HOMES, bid_body, 0, unroll=max(1, UNROLL_P // owners))
    for at, m in enumerate(wanted):
        for b in range(IB_DEV):
            total = jnp.sum(pacc[m * IB_DEV + b], axis=0, keepdims=True)
            if last:
                price_out[at, pl.ds(b, 1), :] = total
            else:
                price_out[pl.ds(m * IB_DEV + b, 1), :] = total


UNROLL_P = 32
UNROLL_V = 32
JOIN = 2
NEAR, FAR = (2, 4), (6, 1)
FOLDED = True
DIRECT = False
UNROLL_B = 32
UNROLL_E = 32


def shaped(shape, dtype=F32):
    return jax.ShapeDtypeStruct(shape, dtype)


PRICE = (HOMES * IB_DEV, BLK)
PARTIAL = pltpu.VMEM((HOMES * IB_DEV + 1, 8, BLK), F32)
GRANT = pltpu.CompilerParams(vmem_limit_bytes=LIMIT)


def run_pack(*operands):
    operands = [pltpu.with_memory_space_constraint(x, pltpu.HBM) for x in operands]
    return pl.pallas_call(
        pack_kernel,
        out_shape=[shaped((WIDE + NOTES, EMB), BF16), shaped((WIDE, EMB), BF16)],
        in_specs=[pl.BlockSpec(memory_space=pltpu.HBM)] * 4,
        out_specs=[VMEM] * 2,
        scratch_shapes=[
            pltpu.VMEM((WIDE,), jnp.int32),
            pltpu.VMEM((1, HOMES), jnp.int32),
            pltpu.SemaphoreType.DMA((4,)),
        ],
        compiler_params=GRANT,
        name="pack",
    )(*operands)


def run_values(adv, arrivals, last, *operands):
    own = arrivals is not None
    count = len(adv)
    columns = (count * AB_DEV, BLK, BLK)
    outs = [
        shaped((count * HOMES, BLK, BLK)),
        shaped(columns),
        shaped(columns),
        shaped(PRICE),
        shaped((8, BLK), jnp.int32),
    ]
    homes = (HOMES * WIDE, EMB)
    scratch = [
        pltpu.SMEM((8, BLK), jnp.int32),
        pltpu.SemaphoreType.DMA,
        pltpu.VMEM((count * AB_DEV + 1, BLK, BLK), F32),
        PARTIAL,
    ]
    if own and last:
        scratch.insert(0, pltpu.VMEM(homes, BF16))
    elif own:
        outs.append(shaped(homes, BF16))
    return pl.pallas_call(
        functools.partial(value_kernel, count, arrivals),
        out_shape=outs,
        in_specs=[VMEM] * (count + len(operands)),
        out_specs=[VMEM] * len(outs),
        scratch_shapes=scratch,
        compiler_params=GRANT,
    )(*adv, *operands)


def run_update(sizes, last, codes, values, spends, spans, parts, wanted, before):
    owners = sum(sizes)
    rows = owners * AB_DEV
    columns = (rows, BLK, BLK)
    tiles = (owners * HOMES, BLK, BLK)
    if last:
        outs = [shaped((AB_DEV, 8, BLK)), shaped((len(wanted), IB_DEV, BLK))]
        scratch = [pltpu.VMEM(tiles, F32)]
        extra = [pltpu.VMEM(columns, F32)]
    else:
        outs = [shaped(columns), shaped(PRICE), shaped(tiles)]
        scratch = extra = []
    operands = [*values, *spends, *parts, *before]
    return pl.pallas_call(
        functools.partial(update_kernel, sizes, last, spans, wanted),
        out_shape=outs,
        in_specs=[SMEM] * len(sizes) + [VMEM] * len(operands),
        out_specs=[VMEM] * len(outs),
        scratch_shapes=[
            *scratch,
            pltpu.VMEM((rows + 1, BLK, BLK), F32),
            *extra,
            pltpu.VMEM(PRICE, F32),
            PARTIAL,
        ],
        compiler_params=GRANT,
        name="last_update" if last else "update",
    )(*codes, *operands)


def move(x, *masks, cores=(0, 1), flip=0):
    if len(masks) == 1:
        masks = masks * 2
    perm = [
        (i * 2 + c, (i ^ masks[c]) * 2 + (c ^ flip)) for i in range(HOMES) for c in cores
    ]
    return lax.ppermute(x, ("imp", "adv"), perm)


def spread(x):
    held = {0: x}
    high = [m for m in REP if m != 1]
    for pick in range(1, 1 << len(high)):
        d = functools.reduce(lambda a, j: a ^ (high[j] if pick >> j & 1 else 0), range(len(high)), 0)
        held[d] = move(x, d)
    if 1 in REP:
        for d in list(held):
            held[d ^ 1] = move(held[d], 1)
    return held


def exchange(price, split):
    for b in split[1:]:
        shape = (HOMES // (2 * b), 2, b * IB_DEV, BLK)
        price = price + move(price, b).reshape(shape)[:, ::-1].reshape(PRICE)
    if not split:
        return (0, 0), [price, move(price, 0, flip=1)]
    b = split[0]
    if JOIN == 0:
        price = price + move(price, 0, flip=1)
        return (0, b), [price, move(price, b)]
    if JOIN == 1:
        shape = (HOMES // (2 * b), 2, b * IB_DEV, BLK)
        price = price + move(price, b).reshape(shape)[:, ::-1].reshape(PRICE)
        return (0, 0), [price, move(price, 0, flip=1)]
    here = [price, move(price, 0, flip=1)]
    there = [move(price, b), move(price, b, flip=1)]
    return (0, 0, b, b), here + there


def small_body(imp_emb, adv_emb, allowances, eligible_slots):
    split = [b for b in (1, 2, 4) if b not in REP]
    packed, imp_own = run_pack(adv_emb, allowances, eligible_slots, imp_emb)
    adv = spread(packed)
    near = move(imp_emb, *NEAR)
    far = move(imp_emb, *FAR)
    near_x = move(near, 1)
    far_x = move(far, 1, cores=(0,))
    blocks = [
        near, move(near, 0, flip=1), far, move(far, 0, flip=1), near_x, move(near_x, 0, flip=1)
    ]
    if DIRECT:
        tail = move(far, 1, cores=(0,), flip=1)
    else:
        tail = move(far_x, 0, cores=(0,), flip=1)
    arrivals = [NEAR, NEAR[::-1], FAR, FAR[::-1]]
    arrivals += [tuple(d ^ 1 for d in pair) for pair in arrivals[:2]]
    blocks.append(jnp.where(lax.axis_index("adv") == 0, far_x, tail))
    arrivals.append((FAR[0] ^ 1, FAR[0] ^ 1))
    values, spends, firsts, codes, price, homes = [], [], [], [], None, None
    for group in GROUPS:
        first = homes is None
        v, sp, f, price, c, *rest = run_values(
            [adv[d] for d in group],
            tuple(arrivals) if first else None,
            group is GROUPS[-1],
            *((imp_own, *blocks) if first else (homes, price)),
        )
        homes = rest[0] if rest else homes
        values.append(v)
        spends.append(sp)
        firsts.append(f)
        codes.append(c)
    sizes = tuple(len(group) for group in GROUPS)
    before = firsts
    for t in range(ITERS):
        last = t == ITERS - 1
        spans, parts = exchange(price, split)
        wanted = (0, *split) if last else tuple(range(HOMES))
        fresh, price, *earned = run_update(
            sizes, last, codes, values, spends, spans, parts, wanted, before
        )
        before = [*earned, fresh]
    utility = jnp.sum(fresh, axis=1)
    here = price[0]
    terms = [here, move(here, 0, flip=1)]
    for at, b in enumerate(split, 1):
        there = price[at]
        terms.append(move(there, b))
        terms.append(move(there, b, flip=1))
    while len(terms) > 1:
        terms = [terms[i] + terms[i + 1] for i in range(0, len(terms), 2)]
    return terms[0].reshape(IB_DEV * BLK), utility.reshape(AB_DEV * BLK)


def small_local(*args):
    return small_body(*args)


def large_local(imp_emb, adv_emb, allowances, eligible_slots):
    slot_count = eligible_slots.shape[1]
    adv_blocks = adv_emb.shape[0] // BLK
    slot_codes = eligible_slots[0]
    is_live = slot_codes >= 0
    clamped = jnp.maximum(slot_codes, 0)
    adv_pick = clamped // IB_DEV
    imp_pick = clamped % IB_DEV
    wanted = jnp.where(is_live, imp_pick, -1)
    cached = []

    def asked_blocks():
        if not cached:
            cached.append(lax.all_to_all(wanted, "imp", split_axis=0, concat_axis=0, tiled=True))
        return cached[0]

    adv_rows = jnp.take(adv_emb.reshape(adv_blocks, BLK, EMB), adv_pick, axis=0)
    score_scale = 1.0 / math.sqrt(EMB)
    asked = asked_blocks()
    home_slabs = imp_emb.reshape(IB_DEV, BLK, EMB)
    chosen = jnp.take(home_slabs, jnp.maximum(asked, 0), axis=0)
    outgoing = jnp.where((asked >= 0)[:, None, None], chosen, jnp.zeros_like(chosen))
    scores = (
        jnp.einsum(
            "nae,nbe->nab",
            adv_rows,
            lax.all_to_all(outgoing, "imp", split_axis=0, concat_axis=0, tiled=True),
            preferred_element_type=jnp.float32,
        )
        * score_scale
    )
    value_tiles = jnp.where(is_live[:, None, None], jax.nn.softplus(scores), 0.0).astype(
        jnp.bfloat16
    )
    highest = lax.Precision.HIGHEST
    spend_rows = allowances.astype(jnp.float32).reshape(adv_blocks, BLK) / 1024.0
    block_ids = jnp.arange(adv_blocks, dtype=jnp.int32)
    picker = (adv_pick[:, None] == block_ids[None, :]).astype(jnp.float32)
    live_picker = picker * is_live[:, None].astype(jnp.float32)
    row_totals = jnp.sum(value_tiles, axis=2, dtype=jnp.float32)
    value_sums = jnp.einsum("nk,na->ka", live_picker, row_totals, precision=highest)
    slot_spend = jnp.einsum("nk,ka->na", live_picker, spend_rows, precision=highest)
    slot_sums = jnp.einsum("nk,ka->na", picker, value_sums, precision=highest)
    bid_tiles = (slot_spend / slot_sums)[:, :, None] * value_tiles
    home_ids = jnp.arange(IB_DEV, dtype=jnp.int32)
    utility = jnp.zeros((adv_blocks, BLK), jnp.float32)
    home_prices = jnp.zeros((IB_DEV, BLK), jnp.float32)
    slot_prices = jnp.zeros((slot_count, BLK), jnp.float32)
    for round_index in range(ITERS + 1):
        totals = jnp.sum(bid_tiles, axis=1)
        asked = asked_blocks()
        asked_picker = (asked[:, None] == home_ids[None, :]).astype(jnp.float32)
        arrived = lax.all_to_all(totals, "imp", split_axis=0, concat_axis=0, tiled=True)
        partial_value = jnp.einsum("ok,oj->kj", asked_picker, arrived, precision=highest)
        home_prices = lax.psum(partial_value, "adv")
        if round_index < ITERS:
            returned = jnp.einsum("ok,kj->oj", asked_picker, home_prices, precision=highest)
            slot_prices = lax.all_to_all(returned, "imp", split_axis=0, concat_axis=0, tiled=True)
        if round_index < ITERS:
            divisor = jnp.where(is_live[:, None], slot_prices, 1.0)
            shares = bid_tiles / divisor[:, None, :]
            earned = value_tiles * shares
            utility = jnp.einsum(
                "nk,na->ka", live_picker, jnp.sum(earned, axis=2), precision=highest
            )
            slot_utility = jnp.einsum("nk,ka->na", picker, utility, precision=highest)
            bid_tiles = (slot_spend / slot_utility)[:, :, None] * earned
    return (home_prices.reshape(IB_DEV * BLK), utility.reshape(adv_blocks * BLK))


def solution(mesh):
    small = mesh.shape["imp"] == HOMES and mesh.shape["adv"] == 2
    return jax.shard_map(
        small_local if small else large_local,
        mesh=mesh,
        in_specs=(
            P(("groups", "imp"), None),
            P(("groups", "imp", "adv"), None),
            P(("groups", "imp", "adv")),
            P(("groups", "imp", "adv"), None),
        ),
        out_specs=(P(("groups", "imp")), P(("groups", "imp", "adv"))),
        check_vma=False,
    )
```

```python
import functools
import math

import jax
import jax.numpy as jnp
from jax import lax
from jax.experimental import pallas as pl
from jax.experimental.pallas import tpu as pltpu
from jax.sharding import PartitionSpec as P

BLK = 128
EMB = 256
IB_DEV = 2
AB_DEV = 2
ITERS = 2
HOMES = 8
WIDE = IB_DEV * BLK
NOTES = 16
REP = (2, 4)
GROUPS = ((0, 2, 4, 6),)

F32 = jnp.float32
BF16 = jnp.bfloat16
SMEM = pl.BlockSpec(memory_space=pltpu.SMEM)
VMEM = pl.BlockSpec(memory_space=pltpu.VMEM)
LIMIT = 12 << 20


def take(refs, *counts):
    parts = []
    for n in counts:
        parts.append(refs[:n])
        refs = refs[n:]
    return (*parts, refs)


def make_eye():
    return lax.broadcasted_iota(jnp.int32, (BLK, BLK), 0) == lax.broadcasted_iota(
        jnp.int32, (BLK, BLK), 1
    )


def softplus(dot):
    scale = 1.0 / math.sqrt(EMB)
    s = dot * scale
    if FOLDED:
        e = jnp.exp2(jnp.abs(dot) * (-scale / math.log(2.0)))
    else:
        e = jnp.exp(-jnp.abs(s))
    near = e - (0.5 * e) * e
    return jnp.maximum(s, 0.0) + jnp.where(e < 0.001, near, jnp.log(1.0 + e))


def fold(tile):
    return jnp.sum(tile.reshape(BLK // 8, 8, BLK), axis=0)


def slot_of(codes, home, owner, owners):
    code = codes[lax.bitwise_xor(lax.axis_index("imp"), home)]
    clamped = jnp.maximum(code, 0)
    k, b = lax.shift_right_logical(clamped, 1), lax.bitwise_and(clamped, 1)
    live = code >= 0
    row = jnp.where(live, owner * AB_DEV + k, owners * AB_DEV)
    return k, b, row, jnp.where(live, home * IB_DEV + b, HOMES * IB_DEV)


def row_block(ref, index):
    return ref[pl.ds(pl.multiple_of(index * BLK, BLK), BLK), :]


def gather_homes(imp_s, core, own, arrived):
    imp_s[pl.ds(0, WIDE), :] = own[...]
    for first, second, ref in arrived:
        d = jnp.where(core == 0, first, second)
        imp_s[pl.ds(pl.multiple_of(d * WIDE, WIDE), WIDE), :] = ref[...]


def pack_kernel(adv, allow, slots, imp, adv_out, imp_out, allow_s, slots_s, sems):
    moves = [
        pltpu.make_async_copy(allow, allow_s, sems.at[0]),
        pltpu.make_async_copy(slots, slots_s, sems.at[1]),
        pltpu.make_async_copy(adv, adv_out.at[pl.ds(0, WIDE), :], sems.at[2]),
        pltpu.make_async_copy(imp, imp_out, sems.at[3]),
    ]
    for move in moves:
        move.start()
    for move in moves[:2]:
        move.wait()
    spend = allow_s[...].reshape(1, WIDE)
    codes = jnp.concatenate([slots_s[...], jnp.zeros((1, WIDE - HOMES), jnp.int32)], axis=1)
    rows = [
        lax.shift_right_logical(spend, 7),
        lax.bitwise_and(spend, 127),
        codes,
        jnp.zeros((NOTES - 3, WIDE), jnp.int32),
    ]
    note = jnp.concatenate(rows, axis=0).astype(F32).astype(BF16)
    adv_out[pl.ds(WIDE, NOTES), :] = note
    for move in moves[2:]:
        move.wait()


def score(lhs, rhs):
    return lax.dot_general(lhs, rhs, (((1,), (1,)), ((), ())), preferred_element_type=F32)


def value_kernel(count, arrivals, *refs):
    own = arrivals is not None
    adv, refs = take(refs, count)
    eye = make_eye()
    if own:
        imp_own, *blocks = refs[: 1 + len(arrivals)]
        refs = refs[1 + len(arrivals) :]
        values, spend_out, factor_out, price_out, code_out, imp_s, table, sem, acc, pacc = refs
    else:
        imp_s, price_in, *refs = refs
        values, spend_out, factor_out, price_out, code_out, table, sem, acc, pacc = refs
    notes = [adv[o][pl.ds(WIDE, NOTES), :].astype(F32) for o in range(count)]
    for o in range(count):
        code_out[pl.ds(o, 1), :] = notes[o][2:3, :BLK].astype(jnp.int32)
    copy = pltpu.make_async_copy(code_out, table, sem)
    copy.start()
    if own:
        core = lax.axis_index("adv")
        gather_homes(imp_s, core, imp_own, [(*d, r) for d, r in zip(arrivals, blocks)])
        pacc[...] = jnp.zeros_like(pacc)
    else:
        for row in range(HOMES * IB_DEV):
            pacc[row] = jnp.concatenate(
                [price_in[pl.ds(row, 1), :], jnp.zeros((7, BLK), F32)], axis=0
            )
    for o in range(count):
        spending = (notes[o][0:1] * 128.0 + notes[o][1:2]) * (1.0 / 1024.0)
        for k in range(AB_DEV):
            row = spending[:, k * BLK : (k + 1) * BLK]
            col = jnp.sum(jnp.where(eye, row, 0.0), axis=1, keepdims=True)
            spend_out[o * AB_DEV + k] = jnp.broadcast_to(col, (BLK, BLK))
    copy.wait()
    codes = [table.at[o] for o in range(count)]
    acc[...] = jnp.zeros_like(acc)

    def value_body(m, carry):
        for o in range(count):
            k, b, row, _ = slot_of(codes[o], m, o, count)
            s = score(row_block(adv[o], k), row_block(imp_s, m * IB_DEV + b))
            v = softplus(s).astype(BF16).astype(F32)
            values[o * HOMES + m] = v
            acc[row] += v
        return carry

    lax.fori_loop(0, HOMES, value_body, 0, unroll=max(1, UNROLL_V // count))
    for r in range(count * AB_DEV):
        total = jnp.sum(acc[r], axis=1, keepdims=True)
        factor_out[r] = spend_out[r] / total

    def bid_body(m, carry):
        for o in range(count):
            k, _, _, row = slot_of(codes[o], m, o, count)
            pacc[row] += fold(factor_out[o * AB_DEV + k] * values[o * HOMES + m])
        return carry

    lax.fori_loop(0, HOMES, bid_body, 0, unroll=max(1, UNROLL_B // count))
    for row in range(HOMES * IB_DEV):
        price_out[pl.ds(row, 1), :] = jnp.sum(pacc[row], axis=0, keepdims=True)


def add_prices(parts):
    rows = []
    for m in range(HOMES):
        terms = [ref[pl.ds((m ^ d) * IB_DEV, IB_DEV), :] for d, ref in parts]
        while len(terms) > 1:
            terms = [terms[i] + terms[i + 1] for i in range(0, len(terms), 2)]
        rows.append(terms[0])
    return jnp.concatenate(rows, axis=0)


def update_kernel(sizes, last, spans, wanted, *refs):
    owners, groups = sum(sizes), len(sizes)
    codes, values, spends, parts, refs = take(refs, groups, groups, groups, len(spans))
    place = [(g, o) for g, n in enumerate(sizes) for o in range(n)]
    refs, (tables, sems) = refs[:-2], refs[-2:]
    copies = [
        pltpu.make_async_copy(codes[g], tables.at[g], sems.at[g]) for g in range(groups)
    ]
    for copy in copies:
        copy.start()
    codes = [tables.at[g, o] for g, o in place]
    if last:
        before, factors, utility_out, price_out, earned_s, acc, fac, rps, pacc = refs
    else:
        firsts, refs = take(refs, groups)
        fac, price_out, earned_s, acc, rps, pacc = refs
    full = add_prices(list(zip(spans, parts)))
    rps[...] = jnp.where(full > 0.0, 1.0 / full, 1.0)
    acc[...] = jnp.zeros_like(acc)
    pacc[...] = jnp.zeros_like(pacc)
    for copy in copies:
        copy.wait()

    def earn_body(m, carry):
        for o, (g, at) in enumerate(place):
            k, b, row, _ = slot_of(codes[o], m, o, owners)
            v = values[g][at * HOMES + m]
            if last:
                bid = factors[o * AB_DEV + k] * before[o * HOMES + m]
            else:
                bid = firsts[g][at * AB_DEV + k] * v
            earned = v * (bid * rps[pl.ds(m * IB_DEV + b, 1), :])
            earned_s[o * HOMES + m] = earned
            acc[row] += earned
        return carry

    lax.fori_loop(0, HOMES, earn_body, 0, unroll=max(1, UNROLL_E // owners))
    for r in range(owners * AB_DEV):
        g, at = place[r // AB_DEV]
        utility = jnp.sum(acc[r], axis=1, keepdims=True)
        fac[r] = spends[g][at * AB_DEV + r % AB_DEV] / utility
        if last and r < AB_DEV:
            utility_out[r] = fold(jnp.where(make_eye(), utility, 0.0))

    def bid_body(m, carry):
        for o in range(owners):
            k, _, _, row = slot_of(codes[o], m, o, owners)
            pacc[row] += fold(fac[o * AB_DEV + k] * earned_s[o * HOMES + m])
        return carry

    if last:
        for m in wanted:
            bid_body(m, 0)
    else:
        lax.fori_loop(0, HOMES, bid_body, 0, unroll=max(1, UNROLL_P // owners))
    for at, m in enumerate(wanted):
        for b in range(IB_DEV):
            total = jnp.sum(pacc[m * IB_DEV + b], axis=0, keepdims=True)
            if last:
                price_out[at, pl.ds(b, 1), :] = total
            else:
                price_out[pl.ds(m * IB_DEV + b, 1), :] = total


UNROLL_P = 32
UNROLL_V = 32
JOIN = 2
NEAR, FAR = (2, 4), (6, 1)
FOLDED = True
DIRECT = False
UNROLL_B = 32
UNROLL_E = 32


def shaped(shape, dtype=F32):
    return jax.ShapeDtypeStruct(shape, dtype)


PRICE = (HOMES * IB_DEV, BLK)
PARTIAL = pltpu.VMEM((HOMES * IB_DEV + 1, 8, BLK), F32)
GRANT = pltpu.CompilerParams(vmem_limit_bytes=LIMIT)


def run_pack(*operands):
    operands = [pltpu.with_memory_space_constraint(x, pltpu.HBM) for x in operands]
    return pl.pallas_call(
        pack_kernel,
        out_shape=[shaped((WIDE + NOTES, EMB), BF16), shaped((WIDE, EMB), BF16)],
        in_specs=[pl.BlockSpec(memory_space=pltpu.HBM)] * 4,
        out_specs=[VMEM] * 2,
        scratch_shapes=[
            pltpu.VMEM((WIDE,), jnp.int32),
            pltpu.VMEM((1, HOMES), jnp.int32),
            pltpu.SemaphoreType.DMA((4,)),
        ],
        compiler_params=GRANT,
        name="pack",
    )(*operands)


def run_values(adv, arrivals, last, *operands):
    own = arrivals is not None
    count = len(adv)
    columns = (count * AB_DEV, BLK, BLK)
    outs = [
        shaped((count * HOMES, BLK, BLK)),
        shaped(columns),
        shaped(columns),
        shaped(PRICE),
        shaped((8, BLK), jnp.int32),
    ]
    homes = (HOMES * WIDE, EMB)
    scratch = [
        pltpu.SMEM((8, BLK), jnp.int32),
        pltpu.SemaphoreType.DMA,
        pltpu.VMEM((count * AB_DEV + 1, BLK, BLK), F32),
        PARTIAL,
    ]
    if own and last:
        scratch.insert(0, pltpu.VMEM(homes, BF16))
    elif own:
        outs.append(shaped(homes, BF16))
    return pl.pallas_call(
        functools.partial(value_kernel, count, arrivals),
        out_shape=outs,
        in_specs=[VMEM] * (count + len(operands)),
        out_specs=[VMEM] * len(outs),
        scratch_shapes=scratch,
        compiler_params=GRANT,
    )(*adv, *operands)


def run_update(sizes, last, codes, values, spends, spans, parts, wanted, before):
    owners = sum(sizes)
    rows = owners * AB_DEV
    columns = (rows, BLK, BLK)
    tiles = (owners * HOMES, BLK, BLK)
    if last:
        outs = [shaped((AB_DEV, 8, BLK)), shaped((len(wanted), IB_DEV, BLK))]
        scratch = [pltpu.VMEM(tiles, F32)]
        extra = [pltpu.VMEM(columns, F32)]
    else:
        outs = [shaped(columns), shaped(PRICE), shaped(tiles)]
        scratch = extra = []
    operands = [*values, *spends, *parts, *before]
    return pl.pallas_call(
        functools.partial(update_kernel, sizes, last, spans, wanted),
        out_shape=outs,
        in_specs=[VMEM] * (len(sizes) + len(operands)),
        out_specs=[VMEM] * len(outs),
        scratch_shapes=[
            *scratch,
            pltpu.VMEM((rows + 1, BLK, BLK), F32),
            *extra,
            pltpu.VMEM(PRICE, F32),
            PARTIAL,
            pltpu.SMEM((len(sizes), 8, BLK), jnp.int32),
            pltpu.SemaphoreType.DMA((len(sizes),)),
        ],
        compiler_params=GRANT,
        name="last_update" if last else "update",
    )(*codes, *operands)


def move(x, *masks, cores=(0, 1), flip=0):
    if len(masks) == 1:
        masks = masks * 2
    perm = [
        (i * 2 + c, (i ^ masks[c]) * 2 + (c ^ flip)) for i in range(HOMES) for c in cores
    ]
    return lax.ppermute(x, ("imp", "adv"), perm)


def spread(x):
    held = {0: x}
    high = [m for m in REP if m != 1]
    for pick in range(1, 1 << len(high)):
        d = functools.reduce(lambda a, j: a ^ (high[j] if pick >> j & 1 else 0), range(len(high)), 0)
        held[d] = move(x, d)
    if 1 in REP:
        for d in list(held):
            held[d ^ 1] = move(held[d], 1)
    return held


def exchange(price, split):
    for b in split[1:]:
        shape = (HOMES // (2 * b), 2, b * IB_DEV, BLK)
        price = price + move(price, b).reshape(shape)[:, ::-1].reshape(PRICE)
    if not split:
        return (0, 0), [price, move(price, 0, flip=1)]
    b = split[0]
    if JOIN == 0:
        price = price + move(price, 0, flip=1)
        return (0, b), [price, move(price, b)]
    if JOIN == 1:
        shape = (HOMES // (2 * b), 2, b * IB_DEV, BLK)
        price = price + move(price, b).reshape(shape)[:, ::-1].reshape(PRICE)
        return (0, 0), [price, move(price, 0, flip=1)]
    here = [price, move(price, 0, flip=1)]
    there = [move(price, b), move(price, b, flip=1)]
    return (0, 0, b, b), here + there


def small_body(imp_emb, adv_emb, allowances, eligible_slots):
    split = [b for b in (1, 2, 4) if b not in REP]
    packed, imp_own = run_pack(adv_emb, allowances, eligible_slots, imp_emb)
    adv = spread(packed)
    near = move(imp_emb, *NEAR)
    far = move(imp_emb, *FAR)
    near_x = move(near, 1)
    far_x = move(far, 1, cores=(0,))
    blocks = [
        near, move(near, 0, flip=1), far, move(far, 0, flip=1), near_x, move(near_x, 0, flip=1)
    ]
    if DIRECT:
        tail = move(far, 1, cores=(0,), flip=1)
    else:
        tail = move(far_x, 0, cores=(0,), flip=1)
    arrivals = [NEAR, NEAR[::-1], FAR, FAR[::-1]]
    arrivals += [tuple(d ^ 1 for d in pair) for pair in arrivals[:2]]
    blocks.append(jnp.where(lax.axis_index("adv") == 0, far_x, tail))
    arrivals.append((FAR[0] ^ 1, FAR[0] ^ 1))
    values, spends, firsts, codes, price, homes = [], [], [], [], None, None
    for group in GROUPS:
        first = homes is None
        v, sp, f, price, c, *rest = run_values(
            [adv[d] for d in group],
            tuple(arrivals) if first else None,
            group is GROUPS[-1],
            *((imp_own, *blocks) if first else (homes, price)),
        )
        homes = rest[0] if rest else homes
        values.append(v)
        spends.append(sp)
        firsts.append(f)
        codes.append(c)
    sizes = tuple(len(group) for group in GROUPS)
    before = firsts
    for t in range(ITERS):
        last = t == ITERS - 1
        spans, parts = exchange(price, split)
        wanted = (0, *split) if last else tuple(range(HOMES))
        fresh, price, *earned = run_update(
            sizes, last, codes, values, spends, spans, parts, wanted, before
        )
        before = [*earned, fresh]
    utility = jnp.sum(fresh, axis=1)
    here = price[0]
    terms = [here, move(here, 0, flip=1)]
    for at, b in enumerate(split, 1):
        there = price[at]
        terms.append(move(there, b))
        terms.append(move(there, b, flip=1))
    while len(terms) > 1:
        terms = [terms[i] + terms[i + 1] for i in range(0, len(terms), 2)]
    return terms[0].reshape(IB_DEV * BLK), utility.reshape(AB_DEV * BLK)


def small_local(*args):
    return small_body(*args)


def large_local(imp_emb, adv_emb, allowances, eligible_slots):
    slot_count = eligible_slots.shape[1]
    adv_blocks = adv_emb.shape[0] // BLK
    slot_codes = eligible_slots[0]
    is_live = slot_codes >= 0
    clamped = jnp.maximum(slot_codes, 0)
    adv_pick = clamped // IB_DEV
    imp_pick = clamped % IB_DEV
    wanted = jnp.where(is_live, imp_pick, -1)
    cached = []

    def asked_blocks():
        if not cached:
            cached.append(lax.all_to_all(wanted, "imp", split_axis=0, concat_axis=0, tiled=True))
        return cached[0]

    adv_rows = jnp.take(adv_emb.reshape(adv_blocks, BLK, EMB), adv_pick, axis=0)
    score_scale = 1.0 / math.sqrt(EMB)
    asked = asked_blocks()
    home_slabs = imp_emb.reshape(IB_DEV, BLK, EMB)
    chosen = jnp.take(home_slabs, jnp.maximum(asked, 0), axis=0)
    outgoing = jnp.where((asked >= 0)[:, None, None], chosen, jnp.zeros_like(chosen))
    scores = (
        jnp.einsum(
            "nae,nbe->nab",
            adv_rows,
            lax.all_to_all(outgoing, "imp", split_axis=0, concat_axis=0, tiled=True),
            preferred_element_type=jnp.float32,
        )
        * score_scale
    )
    value_tiles = jnp.where(is_live[:, None, None], jax.nn.softplus(scores), 0.0).astype(
        jnp.bfloat16
    )
    highest = lax.Precision.HIGHEST
    spend_rows = allowances.astype(jnp.float32).reshape(adv_blocks, BLK) / 1024.0
    block_ids = jnp.arange(adv_blocks, dtype=jnp.int32)
    picker = (adv_pick[:, None] == block_ids[None, :]).astype(jnp.float32)
    live_picker = picker * is_live[:, None].astype(jnp.float32)
    row_totals = jnp.sum(value_tiles, axis=2, dtype=jnp.float32)
    value_sums = jnp.einsum("nk,na->ka", live_picker, row_totals, precision=highest)
    slot_spend = jnp.einsum("nk,ka->na", live_picker, spend_rows, precision=highest)
    slot_sums = jnp.einsum("nk,ka->na", picker, value_sums, precision=highest)
    bid_tiles = (slot_spend / slot_sums)[:, :, None] * value_tiles
    home_ids = jnp.arange(IB_DEV, dtype=jnp.int32)
    utility = jnp.zeros((adv_blocks, BLK), jnp.float32)
    home_prices = jnp.zeros((IB_DEV, BLK), jnp.float32)
    slot_prices = jnp.zeros((slot_count, BLK), jnp.float32)
    for round_index in range(ITERS + 1):
        totals = jnp.sum(bid_tiles, axis=1)
        asked = asked_blocks()
        asked_picker = (asked[:, None] == home_ids[None, :]).astype(jnp.float32)
        arrived = lax.all_to_all(totals, "imp", split_axis=0, concat_axis=0, tiled=True)
        partial_value = jnp.einsum("ok,oj->kj", asked_picker, arrived, precision=highest)
        home_prices = lax.psum(partial_value, "adv")
        if round_index < ITERS:
            returned = jnp.einsum("ok,kj->oj", asked_picker, home_prices, precision=highest)
            slot_prices = lax.all_to_all(returned, "imp", split_axis=0, concat_axis=0, tiled=True)
        if round_index < ITERS:
            divisor = jnp.where(is_live[:, None], slot_prices, 1.0)
            shares = bid_tiles / divisor[:, None, :]
            earned = value_tiles * shares
            utility = jnp.einsum(
                "nk,na->ka", live_picker, jnp.sum(earned, axis=2), precision=highest
            )
            slot_utility = jnp.einsum("nk,ka->na", picker, utility, precision=highest)
            bid_tiles = (slot_spend / slot_utility)[:, :, None] * earned
    return (home_prices.reshape(IB_DEV * BLK), utility.reshape(adv_blocks * BLK))


def solution(mesh):
    small = mesh.shape["imp"] == HOMES and mesh.shape["adv"] == 2
    return jax.shard_map(
        small_local if small else large_local,
        mesh=mesh,
        in_specs=(
            P(("groups", "imp"), None),
            P(("groups", "imp", "adv"), None),
            P(("groups", "imp", "adv")),
            P(("groups", "imp", "adv"), None),
        ),
        out_specs=(P(("groups", "imp")), P(("groups", "imp", "adv"))),
        check_vma=False,
    )
```
